32 devices in a mesh: grp: 4 (over x, core), row: 8 (over z, y).
Axes of the slice: x: 2, y: 2, z: 4, core: 2. Of those that a mesh axis runs over, the one named last changes fastest.
Arguments:
- signal: bfloat16 [128, 64, 128], P(('grp', 'row')), may hold values from -6 to 6
- leaf_basis: bfloat16 [128, 64, 128], P(('grp', 'row')), may hold values from -0.5 to 0.5
- near_blocks: bfloat16 [128, 3, 128, 128], P(('grp', 'row')), may hold values from -0.3125 to 0.3125
- coupling: bfloat16 [6144, 4096], P(('grp', 'row')), may hold values from -0.109375 to 0.109375
- block_cols: int32 [6144], P(('grp', 'row')), may hold values from 0 to 127, as said below
- block_rows: int32 [6144], P(('grp', 'row')), may hold values from 0 to 3
- block_live: int32 [6144], P(('grp', 'row')), may hold values 0 or 1
Outputs:
- product: bfloat16 [128, 64, 128], P(('grp', 'row'))
The draws below stay inside these ranges and needn't reach their ends.
Inputs may be any that keep to these rules, and one draw needn't show every extreme that they name: `block_cols`: slot b of device d (d = b // 192, in group h = d // 8) names a column cluster of group (h + o) mod (4), where o = (b mod 192) // 64 - 1; a group's clusters are g * 32 to (g + 1) * 32 - 1.
All inputs are finite; a program needn't handle non-finite values. No bound on the sum of `block_live` on one device may be relied on, other than what follows from the above.
Results may differ from the reference program's by a relative error of at most 0.0039.
Values may be sent and summed in bfloat16 or wider, within the bound.
No kernel may reach another device: no remote copies, remote signals or barrier semaphores. Data moves between devices by JAX's collectives and lax.ppermute only.
A program may use at most 64 MiB of HBM per device.

```python
import jax
import jax.numpy as jnp
from jax import lax

LEAF = 128
K = 64
R = 64
CL_DEV = 4
BPC = 16
BPG = 64
NBLK_DEV = 192
GC = 32
CLUST = 128
BLOCKS = 6144
DEVICES = 32


def draw_block_cols(key, part):
    slot_ids = jnp.arange(BLOCKS, dtype=jnp.int32)
    device = slot_ids // NBLK_DEV
    offset = slot_ids % NBLK_DEV // BPG - 1
    home_group = device * CL_DEV // GC
    group_count = CLUST // GC
    column_group = (home_group + offset + group_count) % group_count
    within = jax.random.randint(key, (BLOCKS,), 0, GC, dtype=jnp.int32)
    return column_group * GC + within


def plant(values, own_key, low, top_value):
    longest = values.shape.index(max(values.shape))
    spots = []
    for shift in (0, 1):
        where = [jax.random.randint(jax.random.fold_in(own_key, axis), (), 0, length) for axis, length in enumerate(values.shape)]
        where[longest] = (where[longest] + shift) % values.shape[longest]
        spots.append(tuple(where))
    return values.at[spots[0]].set(low).at[spots[1]].set(top_value)


def level_of(key, shape, shards, least, high):
    level = 1.0
    for position, parts in shards:
        steps = jax.random.uniform(jax.random.fold_in(jax.random.fold_in(key, 6), position), (parts,), jnp.float32, least / len(shards), high / len(shards))
        level = level * jnp.repeat(jnp.exp(steps), shape[position] // parts).reshape((-1,) + (1,) * (len(shape) - 1 - position))
    return level


def bell_draw(key, shape, width, bound, split=(), kind=jnp.bfloat16):
    array = width * jax.random.normal(key, shape, jnp.float32)
    if split:
        array = array * level_of(key, shape, split, -0.22, 0.18)
    return jnp.clip(array, -bound, bound).astype(kind)


def setup_inputs(seed: int = 0) -> dict:
    key_of = jax.random.split(jax.random.key(seed), 8)
    signal = bell_draw(key_of[0], (CLUST, R, LEAF), 1.0, 6.0, ((0, 32),))
    leaf_basis = bell_draw(key_of[1], (CLUST, K, LEAF), LEAF ** -0.5, 0.5, ((0, 32),))
    near_blocks = bell_draw(key_of[2], (CLUST, 3, LEAF, LEAF), (3 * LEAF) ** -0.5, 0.3125, ((0, 32),))
    coupling = bell_draw(key_of[3], (BLOCKS, K * K), (3 * BPC * K) ** -0.5, 0.109375, ((0, 32),))
    block_cols = draw_block_cols(jax.random.fold_in(key_of[7], 71), 0)
    block_rows = plant(jax.random.randint(key_of[5], (BLOCKS,), 0, CL_DEV), jax.random.fold_in(key_of[5], 1), 0, CL_DEV - 1).astype(jnp.int32)
    block_live = plant((jax.random.randint(key_of[6], (BLOCKS,), 0, 4) < 3).astype(jnp.int32), jax.random.fold_in(key_of[6], 1), 0, 1)
    return dict(signal=signal, leaf_basis=leaf_basis, near_blocks=near_blocks, coupling=coupling, block_cols=block_cols, block_rows=block_rows, block_live=block_live)


def reference(signal, leaf_basis, near_blocks, coupling, block_cols, block_rows, block_live):
    skeleton = jnp.einsum('crl,ckl->crk', signal.astype(jnp.float32), leaf_basis.astype(jnp.float32)).astype(jnp.bfloat16)
    blocks_all = coupling.reshape(DEVICES, NBLK_DEV, K, K)
    columns = block_cols.reshape(DEVICES, NBLK_DEV)
    row_ids = block_rows.reshape(DEVICES, NBLK_DEV)
    live_mask = block_live.reshape(DEVICES, NBLK_DEV)
    cluster_ids = jnp.arange(CL_DEV, dtype=jnp.int32)

    def device_far(pieces):
        blocks, cols_here, rows_here, live_here = pieces
        sources = skeleton[cols_here].astype(jnp.float32)
        contrib = jnp.einsum('brm,bkm->brk', sources, blocks.astype(jnp.float32))
        contrib = contrib * live_here.astype(jnp.float32)[:, None, None]
        one_hot = (rows_here[None, :] == cluster_ids[:, None]).astype(jnp.float32)
        return jnp.einsum('cb,brk->crk', one_hot, contrib, precision=lax.Precision.HIGHEST)

    far = lax.map(device_far, (blocks_all, columns, row_ids, live_mask)).reshape(CLUST, R, K)
    far_skeleton = far.astype(jnp.bfloat16)
    total = jnp.einsum('crk,ckl->crl', far_skeleton.astype(jnp.float32), leaf_basis.astype(jnp.float32))
    zero_cluster = jnp.zeros((1, R, LEAF), jnp.bfloat16)
    before = jnp.concatenate([zero_cluster, signal[:-1]], axis=0)
    after = jnp.concatenate([signal[1:], zero_cluster], axis=0)
    for index, neighbour in enumerate([before, signal, after]):
        total = total + jnp.einsum('crl,cml->crm', neighbour.astype(jnp.float32), near_blocks[:, index].astype(jnp.float32))
    return total.astype(jnp.bfloat16)
```

```python
import functools

import jax
import jax.numpy as jnp
from jax import lax
from jax.experimental import pallas as pl
from jax.experimental.pallas import tpu as pltpu
from jax.sharding import PartitionSpec as P

K = 64
R = 64
LANES = 128
HALVES = LANES // K
TILES = K // HALVES


VMEM = pl.BlockSpec(memory_space=pltpu.VMEM)
F32 = jnp.float32
BF16 = jnp.bfloat16


def dot_nt(a, b):
    return lax.dot_general(a, b, (((1,), (1,)), ((), ())), preferred_element_type=F32)


def skeleton_kernel(signal_ref, basis_ref, out_ref):
    for pair in range(signal_ref.shape[0] // 2):
        sides = [
            dot_nt(basis_ref[2 * pair + w], signal_ref[2 * pair + w]).astype(BF16) for w in range(2)
        ]
        out_ref[pl.ds(pair * K, K), :] = jnp.concatenate(sides, axis=1)


def operator_kernel(
    n_grp, n_row, cl_dev, cols_ref, rows_ref, live_ref, coupling_ref, out_ref, wide_ref
):
    gc = n_row * cl_dev
    shift = gc.bit_length() - 1
    local = cl_dev.bit_length() - 1
    n_slots = coupling_ref.shape[0]
    group = lax.axis_index("grp")
    row = lax.axis_index("row")
    cols = cols_ref[...]
    delta = (lax.shift_right_logical(cols, shift) - group + n_grp) & (n_grp - 1)
    partner = jnp.where((group & 1) == 0, 1, n_grp - 1)
    kind = jnp.where(delta == 0, 0, jnp.where(delta == partner, 1, 2))
    place = (cols & (gc - 1)) ^ lax.shift_left(row, local)
    code = kind * (cl_dev * gc) + rows_ref[...] * gc + place
    code = jnp.where(live_ref[...] > 0, code, -1)
    n_codes = 3 * cl_dev * gc
    select = (lax.broadcasted_iota(jnp.int32, (n_codes, n_slots), 0) == code).astype(F32).astype(BF16)

    def spread(step, _):
        lanes = pl.multiple_of(step * 2 * LANES, 2 * LANES)
        summed = jnp.dot(
            select, coupling_ref[:, pl.ds(lanes, 2 * LANES)], preferred_element_type=F32
        )
        for side in range(2):
            t = step * 2 + side
            for kind_row in range(3 * cl_dev):
                kind_here, cluster = divmod(kind_row, cl_dev)
                base = kind_here * gc * cl_dev * TILES + cluster * TILES
                wide_ref[pl.ds(base + t, gc, stride=cl_dev * TILES), :] = summed[
                    kind_row * gc : (kind_row + 1) * gc, side * LANES : (side + 1) * LANES
                ]
        return 0

    lax.fori_loop(0, TILES // 2, spread, 0)
    height = cl_dev * TILES

    def narrow(pair, _):
        for which in range(2):
            start = pl.multiple_of((pair * 2 + which) * height, height)
            out_ref[pair, :, which * LANES : (which + 1) * LANES] = wide_ref[
                pl.ds(start, height), :
            ].astype(BF16)
        return 0

    lax.fori_loop(0, out_ref.shape[0], narrow, 0)


def far_pieces(total, operator_ref, pieces, kinds, n_pairs_kind, pairs_piece):
    lane = lax.broadcasted_iota(jnp.int32, (K, LANES), 1)
    first = lane < K
    for piece_ref, (kind, places) in zip(pieces, kinds):
        for at, place in enumerate(places):
            for pair in range(pairs_piece):
                both = piece_ref[pl.ds((at * pairs_piece + pair) * K, K), :]
                swapped = jnp.concatenate([both[:, K:], both[:, :K]], axis=1)
                zero = jnp.zeros_like(both)
                weights = jnp.concatenate(
                    [
                        jnp.where(first, both, zero),
                        jnp.where(first, zero, swapped),
                        jnp.where(first, swapped, zero),
                        jnp.where(first, zero, both),
                    ],
                    axis=0,
                )
                index = kind * n_pairs_kind + place * pairs_piece + pair
                total = total + jnp.dot(
                    operator_ref[index], weights, preferred_element_type=F32
                )
    return total


def far_kernel(kinds, n_pairs_kind, pairs_piece, started, *refs):
    operator_ref, *rest = refs
    pieces = rest[: len(kinds)]
    out_ref = rest[-1]
    if started:
        total = rest[len(kinds)][...]
    else:
        total = jnp.zeros(out_ref.shape, F32)
    out_ref[...] = far_pieces(total, operator_ref, pieces, kinds, n_pairs_kind, pairs_piece)


def near_kernel(signal_ref, near_ref, basis_ref, total_ref, spread_ref):
    cl_dev = signal_ref.shape[0]
    for c in range(cl_dev):
        total = dot_nt(signal_ref[c], near_ref[c, 1])
        if c > 0:
            total = total + dot_nt(signal_ref[c - 1], near_ref[c, 0])
        if c < cl_dev - 1:
            total = total + dot_nt(signal_ref[c + 1], near_ref[c, 2])
        total_ref[:, c * LANES : (c + 1) * LANES] = total
    spread_ref[...] = jnp.zeros_like(spread_ref)
    for c in range(cl_dev):
        wide = basis_ref[c].astype(F32).reshape(TILES, HALVES, LANES)
        for parity in range(HALVES):
            start = parity * cl_dev * TILES + c * TILES
            spread_ref[start : start + TILES, c * LANES : (c + 1) * LANES] = wide[:, parity].astype(BF16)


def final_kernel(kinds, n_pairs_kind, pairs_piece, n_row, n_grp, operator_ref, *refs):
    pieces = refs[: len(kinds)]
    far_ref, near_total_ref, spread_ref, low_ref, high_ref, near_ref, out_ref = refs[len(kinds) :]
    cl_dev = out_ref.shape[0]
    total = far_pieces(far_ref[...], operator_ref, pieces, kinds, n_pairs_kind, pairs_piece)
    turned = total.T.astype(BF16)
    lhs = jnp.concatenate([turned[p * R : (p + 1) * R] for p in range(HALVES)], axis=1)
    res = near_total_ref[...] + jnp.dot(lhs, spread_ref[...], preferred_element_type=F32)
    for c in range(cl_dev):
        here = res[:, c * LANES : (c + 1) * LANES]
        if c == 0:
            here = here + dot_nt(low_ref[0], near_ref[0, 0])
        if c == cl_dev - 1:
            here = here + dot_nt(high_ref[0], near_ref[cl_dev - 1, 2])
        out_ref[c] = here.astype(BF16)


def per_device(signal, leaf_basis, near_blocks, coupling, block_cols, block_rows, block_live):
    cl_dev = signal.shape[0]
    n_row = lax.axis_size("row")
    n_grp = lax.axis_size("grp")
    n_dev = n_row * n_grp
    gc = cl_dev * n_row
    pairs_piece = cl_dev // 2
    n_pairs_kind = gc // 2
    height = cl_dev * TILES
    shape = jax.ShapeDtypeStruct

    def across_row(value, bit):
        return lax.ppermute(value, "row", [(i, i ^ bit) for i in range(n_row)])

    def to_partner(value):
        return lax.ppermute(value, "grp", [(i, i ^ 1) for i in range(n_grp)])

    def to_other(value):
        pairs = [(i, (i + 1) % n_grp if i % 2 else (i - 1) % n_grp) for i in range(n_grp)]
        return lax.ppermute(value, "grp", pairs)

    mine = pl.pallas_call(
        skeleton_kernel,
        out_shape=shape((cl_dev // 2 * K, LANES), BF16),
        in_specs=[VMEM] * 2,
        out_specs=VMEM,
        name="skeleton",
    )(signal, leaf_basis)

    places = [0]
    panel = mine
    bit = n_row // 2
    while bit > 1:
        panel = jnp.concatenate([panel, across_row(panel, bit)], axis=0)
        places = places + [p ^ bit for p in places]
        bit //= 2
    over_y = across_row(panel, 1)
    places_y = [p ^ 1 for p in places]
    other_a = to_other(panel)
    other_b = to_other(over_y)
    partner = to_partner(jnp.concatenate([panel, over_y], axis=0))

    late_signal, _ = lax.optimization_barrier((signal, panel))
    low = lax.ppermute(late_signal[-1:], ("grp", "row"), [(i, i + 1) for i in range(n_dev - 1)])
    high = lax.ppermute(late_signal[:1], ("grp", "row"), [(i + 1, i) for i in range(n_dev - 1)])

    operator = pl.pallas_call(
        functools.partial(operator_kernel, n_grp, n_row, cl_dev),
        out_shape=shape((3 * n_pairs_kind, height, 2 * LANES), BF16),
        in_specs=[VMEM] * 4,
        out_specs=VMEM,
        scratch_shapes=[pltpu.VMEM((3 * gc * height, LANES), F32)],
        name="operator",
    )(block_cols[None], block_rows[None], block_live[None], coupling)

    near_total, spread = pl.pallas_call(
        near_kernel,
        out_shape=[shape((R, cl_dev * LANES), F32), shape((HALVES * height, cl_dev * LANES), BF16)],
        in_specs=[VMEM] * 3,
        out_specs=[VMEM] * 2,
        name="near",
    )(signal, near_blocks, leaf_basis)

    first_kinds = [(0, places), (0, places_y), (2, places), (1, places + places_y)]
    far = pl.pallas_call(
        functools.partial(far_kernel, first_kinds, n_pairs_kind, pairs_piece, False),
        out_shape=shape((height, LANES), F32),
        in_specs=[VMEM] * (1 + len(first_kinds)),
        out_specs=VMEM,
        name="far",
    )(operator, panel, over_y, other_a, partner)

    last_kinds = [(2, places_y)]
    return pl.pallas_call(
        functools.partial(final_kernel, last_kinds, n_pairs_kind, pairs_piece, n_row, n_grp),
        out_shape=shape(signal.shape, BF16),
        in_specs=[VMEM] * 8,
        out_specs=VMEM,
        name="final",
    )(operator, other_b, far, near_total, spread, low, high, near_blocks)


def solution(mesh):
    in_specs = (
        P(("grp", "row"), None, None),
        P(("grp", "row"), None, None),
        P(("grp", "row"), None, None, None),
        P(("grp", "row"), None),
        P(("grp", "row")),
        P(("grp", "row")),
        P(("grp", "row")),
    )
    out_specs = P(("grp", "row"), None, None)
    return jax.shard_map(
        per_device, mesh=mesh, in_specs=in_specs, out_specs=out_specs, check_vma=False
    )
```

```python
import functools

import jax
import jax.numpy as jnp
from jax import lax
from jax.experimental import pallas as pl
from jax.experimental.pallas import tpu as pltpu
from jax.sharding import PartitionSpec as P


K = 64
R = 64
LANES = 128
HALVES = LANES // K
TILES = K // HALVES
PAD = 4


F32 = jnp.float32
BF16 = jnp.bfloat16


def dot_nt(a, b):
    return lax.dot_general(a, b, (((1,), (1,)), ((), ())), preferred_element_type=F32)


def call(kernel, outs, *args, scratch=(), room=0):
    spec = pl.BlockSpec(memory_space=pltpu.VMEM)
    single = len(outs) == 1
    shapes = [pltpu.VMEM(s, d) for s, d in outs]
    return pl.pallas_call(
        kernel,
        out_shape=shapes[0] if single else shapes,
        in_specs=[spec] * len(args),
        out_specs=spec if single else [spec] * len(outs),
        scratch_shapes=scratch,
        compiler_params=pltpu.CompilerParams(vmem_limit_bytes=room + (2 << 20)),
    )(*args)


def skeleton_kernel(signal_ref, basis_ref, out_ref, across_ref, along_ref):
    last = signal_ref.shape[0] - 1
    for pair in range(signal_ref.shape[0] // 2):
        sides = [
            dot_nt(basis_ref[2 * pair + w], signal_ref[2 * pair + w]).astype(BF16) for w in range(2)
        ]
        out_ref[pl.ds(pair * K, K), :] = jnp.concatenate(sides, axis=1)
    odd = (lax.axis_index("row") & 1) == 1
    across_ref[...] = jnp.where(odd, signal_ref[0], signal_ref[last])
    along_ref[...] = jnp.where(odd, signal_ref[last], signal_ref[0])


def operator_kernel(n_grp, n_row, cl_dev, kinds, cols_ref, rows_ref, live_ref, *refs):
    coupling_ref, out_ref, wide_ref = refs
    gc = n_row * cl_dev
    shift = gc.bit_length() - 1
    local = cl_dev.bit_length() - 1
    n_slots = coupling_ref.shape[0]
    group = lax.axis_index("grp")
    row = lax.axis_index("row")
    cols = cols_ref[...]
    delta = (lax.shift_right_logical(cols, shift) - group + n_grp) & (n_grp - 1)
    partner = jnp.where((group & 1) == 0, 1, n_grp - 1)
    kind = jnp.where(delta == 0, 0, jnp.where(delta == partner, 1, 2)) - kinds[0]
    place = (cols & (gc - 1)) ^ lax.shift_left(row, local)
    code = kind * (cl_dev * gc) + rows_ref[...] * gc + place
    code = jnp.where(live_ref[...] > 0, code, -1)
    n_codes = len(kinds) * cl_dev * gc
    select = (lax.broadcasted_iota(jnp.int32, (n_codes, n_slots), 0) == code).astype(F32).astype(BF16)
    height = cl_dev * TILES
    tall = height + PAD

    def spread(step, _):
        lanes = pl.multiple_of(step * 2 * LANES, 2 * LANES)
        summed = jnp.dot(
            select, coupling_ref[:, pl.ds(lanes, 2 * LANES)], preferred_element_type=F32
        )
        for side in range(2):
            t = step * 2 + side
            for kind_row in range(len(kinds) * cl_dev):
                kind_here, cluster = divmod(kind_row, cl_dev)
                base = kind_here * gc * tall + cluster * TILES
                wide_ref[pl.ds(base + t, gc, stride=tall), :] = summed[
                    kind_row * gc : (kind_row + 1) * gc, side * LANES : (side + 1) * LANES
                ]
        return 0

    lax.fori_loop(0, TILES // 2, spread, 0)

    def narrow(pair, _):
        for which in range(2):
            start = (pair * 2 + which) * tall
            out_ref[pair, :, which * LANES : (which + 1) * LANES] = wide_ref[
                pl.ds(start, height), :
            ].astype(BF16)
        return 0

    lax.fori_loop(0, out_ref.shape[0], narrow, 0)


def far_pieces(total, pieces, pairs_piece):
    lane = lax.broadcasted_iota(jnp.int32, (K, LANES), 1)
    first = lane < K
    for operator_ref, base, piece_ref, places in pieces:
        for at, place in enumerate(places):
            for pair in range(pairs_piece):
                both = piece_ref[pl.ds((at * pairs_piece + pair) * K, K), :]
                swapped = jnp.concatenate([both[:, K:], both[:, :K]], axis=1)
                zero = jnp.zeros_like(both)
                weights = jnp.concatenate(
                    [
                        jnp.where(first, both, zero),
                        jnp.where(first, zero, swapped),
                        jnp.where(first, swapped, zero),
                        jnp.where(first, zero, both),
                    ],
                    axis=0,
                )
                index = base + place * pairs_piece + pair
                total = total + jnp.dot(
                    operator_ref[index], weights, preferred_element_type=F32
                )
    return total


def far_kernel(plan, pairs_piece, started, *refs):
    out_ref = refs[-1]
    total = refs[-2][...] if started else jnp.zeros(out_ref.shape, F32)
    pieces = [(refs[o], base, refs[p], places) for o, base, p, places in plan]
    out_ref[...] = far_pieces(total, pieces, pairs_piece)


def near_kernel(signal_ref, near_ref, basis_ref, total_ref, spread_ref):
    cl_dev = signal_ref.shape[0]
    for c in range(cl_dev):
        total = dot_nt(signal_ref[c], near_ref[c, 1])
        if c > 0:
            total = total + dot_nt(signal_ref[c - 1], near_ref[c, 0])
        if c < cl_dev - 1:
            total = total + dot_nt(signal_ref[c + 1], near_ref[c, 2])
        total_ref[:, c * LANES : (c + 1) * LANES] = total
    spread_ref[...] = jnp.zeros_like(spread_ref)
    for c in range(cl_dev):
        wide = basis_ref[c].astype(F32).reshape(TILES, HALVES, LANES)
        for parity in range(HALVES):
            start = parity * cl_dev * TILES + c * TILES
            spread_ref[start : start + TILES, c * LANES : (c + 1) * LANES] = wide[:, parity].astype(BF16)


def halo_kernel(n_dev, across_ref, along_ref, near_ref, so_far_ref, total_ref):
    cl_dev = near_ref.shape[0]
    row = lax.axis_index("row")
    me = lax.axis_index("grp") * lax.axis_size("row") + row
    odd = (row & 1) == 1
    across = across_ref[...]
    along = along_ref[...]
    zero = jnp.zeros_like(across)
    low = jnp.where(me == 0, zero, jnp.where(odd, across, along))
    high = jnp.where(me == n_dev - 1, zero, jnp.where(odd, along, across))
    total_ref[...] = so_far_ref[...]
    total_ref[:, :LANES] += dot_nt(low, near_ref[0, 0])
    total_ref[:, (cl_dev - 1) * LANES :] += dot_nt(high, near_ref[cl_dev - 1, 2])


def final_kernel(plan, pairs_piece, *refs):
    far_ref, near_total_ref, spread_ref, out_ref = refs[-4:]
    pieces = [(refs[o], base, refs[p], places) for o, base, p, places in plan]
    total = far_pieces(far_ref[...], pieces, pairs_piece)
    turned = total.T.astype(BF16)
    lhs = jnp.concatenate([turned[p * R : (p + 1) * R] for p in range(HALVES)], axis=1)
    res = near_total_ref[...] + jnp.dot(lhs, spread_ref[...], preferred_element_type=F32)
    for c in range(out_ref.shape[0]):
        out_ref[c] = res[:, c * LANES : (c + 1) * LANES].astype(BF16)


def held(*values):
    return [pltpu.with_memory_space_constraint(v, pltpu.VMEM) for v in values]


def after(value, *others):
    return lax.optimization_barrier((value, *others))[0]


def per_device(signal, leaf_basis, near_blocks, coupling, block_cols, block_rows, block_live):
    cl_dev = signal.shape[0]
    n_row = lax.axis_size("row")
    n_grp = lax.axis_size("grp")
    n_dev = n_row * n_grp
    gc = cl_dev * n_row
    pairs_piece = cl_dev // 2
    pairs_kind = gc // 2
    height = cl_dev * TILES

    def across_row(value, bit):
        return lax.ppermute(value, "row", [(i, i ^ bit) for i in range(n_row)])

    signal, leaf_basis, near_blocks, coupling, cols, rows, live = held(
        signal, leaf_basis, near_blocks, coupling, block_cols[None], block_rows[None], block_live[None]
    )
    partners = [(i, i ^ 1) for i in range(n_grp)]
    others = [(i, (i + 1) % n_grp if i % 2 else (i - 1) % n_grp) for i in range(n_grp)]

    mine, for_across, for_along = call(
        skeleton_kernel, [((cl_dev // 2 * K, LANES), BF16), ((R, LANES), BF16), ((R, LANES), BF16)], signal, leaf_basis
    )

    def operator(kinds):
        return call(
            functools.partial(operator_kernel, n_grp, n_row, cl_dev, kinds),
            [((len(kinds) * pairs_kind, height, 2 * LANES), BF16)],
            cols,
            rows,
            live,
            coupling,
            scratch=[pltpu.VMEM((len(kinds) * gc * (height + PAD), LANES), F32)],
            room=len(kinds) * gc * (height + PAD) * LANES * 4,
        )

    own_operator = operator((0,))
    side_operator = operator((1, 2))
    near_total, spread = call(
        near_kernel,
        [((R, cl_dev * LANES), F32), ((HALVES * height, cl_dev * LANES), BF16)],
        signal,
        near_blocks,
        leaf_basis,
    )

    places = [0]
    panel = mine
    bit = n_row // 2
    while bit > 1:
        got = across_row(panel, bit)
        panel = jnp.concatenate([panel, got], axis=0)
        places = places + [p ^ bit for p in places]
        bit //= 2
    over_y = across_row(panel, 1)
    places_y = [p ^ 1 for p in places]
    other_a = lax.ppermute(panel, "grp", others)
    across = across_row(after(for_across, panel), 1)
    pairs = [(i, i + 1) for i in range(1, n_dev - 1, 2)]
    along = lax.ppermute(after(for_along, panel), ("grp", "row"), pairs + [(b, a) for a, b in pairs])
    own_far = call(
        functools.partial(far_kernel, [(0, 0, 1, places)], pairs_piece, False),
        [((height, LANES), F32)],
        own_operator,
        *held(panel),
    )
    other_b = lax.ppermute(over_y, "grp", others)
    partner = lax.ppermute(jnp.concatenate([panel, over_y], axis=0), "grp", partners)

    with_halo = call(
        functools.partial(halo_kernel, n_dev),
        [((R, cl_dev * LANES), F32)],
        *held(across, along),
        near_blocks,
        near_total,
    )
    plan = [(0, 0, 2, places_y), (1, pairs_kind, 3, places), (1, 0, 4, places + places_y)]
    far = call(
        functools.partial(far_kernel, plan, pairs_piece, True),
        [((height, LANES), F32)],
        own_operator,
        side_operator,
        *held(over_y, other_a, partner),
        own_far,
    )
    return pl.pallas_call(
        functools.partial(final_kernel, [(0, pairs_kind, 1, places_y)], pairs_piece),
        out_shape=jax.ShapeDtypeStruct(signal.shape, BF16),
        in_specs=[pl.BlockSpec(memory_space=pltpu.VMEM)] * 5,
        out_specs=pl.BlockSpec(memory_space=pltpu.VMEM),
        compiler_params=pltpu.CompilerParams(vmem_limit_bytes=4 << 20),
        name="final",
    )(side_operator, *held(other_b), far, with_halo, spread)


def solution(mesh):
    in_specs = (
        P(("grp", "row"), None, None),
        P(("grp", "row"), None, None),
        P(("grp", "row"), None, None, None),
        P(("grp", "row"), None),
        P(("grp", "row")),
        P(("grp", "row")),
        P(("grp", "row")),
    )
    out_specs = P(("grp", "row"), None, None)

    return jax.shard_map(per_device, mesh=mesh, in_specs=in_specs, out_specs=out_specs, check_vma=False)
```

```python
import functools

import jax
import jax.numpy as jnp
from jax import lax
from jax.experimental import pallas as pl
from jax.experimental.pallas import tpu as pltpu
from jax.sharding import PartitionSpec as P


K = 64
R = 64
LANES = 128
HALVES = LANES // K
TILES = K // HALVES
PAD = 4


F32 = jnp.float32
BF16 = jnp.bfloat16


def dot_nt(a, b):
    return lax.dot_general(a, b, (((1,), (1,)), ((), ())), preferred_element_type=F32)


def call(kernel, outs, *args, scratch=(), room=0, in_hbm=()):
    spec = pl.BlockSpec(memory_space=pltpu.VMEM)
    far_spec = pl.BlockSpec(memory_space=pltpu.HBM)
    single = len(outs) == 1
    shapes = [pltpu.VMEM(s, d) for s, d in outs]
    args = [
        pltpu.with_memory_space_constraint(a, pltpu.HBM) if i in in_hbm else a
        for i, a in enumerate(args)
    ]
    return pl.pallas_call(
        kernel,
        out_shape=shapes[0] if single else shapes,
        in_specs=[far_spec if i in in_hbm else spec for i in range(len(args))],
        out_specs=spec if single else [spec] * len(outs),
        scratch_shapes=scratch,
        compiler_params=pltpu.CompilerParams(vmem_limit_bytes=room + (2 << 20)),
    )(*args)


def skeleton_kernel(*refs):
    sources, here, (out_ref, across_ref, along_ref, sems) = refs[:5], refs[5:10], refs[10:]
    copies = [pltpu.make_async_copy(a, b, sems.at[n]) for n, (a, b) in enumerate(zip(sources, here))]
    for copy in copies:
        copy.start()
    signal_ref, basis_ref = here[:2]
    copies[0].wait()
    copies[1].wait()
    last = signal_ref.shape[0] - 1
    for pair in range(signal_ref.shape[0] // 2):
        sides = [
            dot_nt(basis_ref[2 * pair + w], signal_ref[2 * pair + w]).astype(BF16) for w in range(2)
        ]
        out_ref[pl.ds(pair * K, K), :] = jnp.concatenate(sides, axis=1)
    odd = (lax.axis_index("row") & 1) == 1
    across_ref[...] = jnp.where(odd, signal_ref[0], signal_ref[last])
    along_ref[...] = jnp.where(odd, signal_ref[last], signal_ref[0])
    for copy in copies[2:]:
        copy.wait()


def slot_codes(n_grp, n_row, cl_dev, first_kind, cols, rows, live):
    gc = n_row * cl_dev
    shift = gc.bit_length() - 1
    local = cl_dev.bit_length() - 1
    group = lax.axis_index("grp")
    row = lax.axis_index("row")
    delta = (lax.shift_right_logical(cols, shift) - group + n_grp) & (n_grp - 1)
    partner = jnp.where((group & 1) == 0, 1, n_grp - 1)
    kind = jnp.where(delta == 0, 0, jnp.where(delta == partner, 1, 2)) - first_kind
    place = (cols & (gc - 1)) ^ lax.shift_left(row, local)
    return jnp.where(live > 0, kind * (cl_dev * gc) + rows * gc + place, -1)


def sum_slots(n_kinds, gc, cl_dev, code, coupling_of, out_ref, wide_ref):
    n_codes = n_kinds * cl_dev * gc
    shape = (n_codes, code.shape[1])
    select = (lax.broadcasted_iota(jnp.int32, shape, 0) == code).astype(F32).astype(BF16)
    height = cl_dev * TILES
    tall = height + PAD
    for step in range(TILES // 2):
        summed = jnp.dot(select, coupling_of(step), preferred_element_type=F32)
        for side in range(2):
            t = step * 2 + side
            for kind_row in range(n_kinds * cl_dev):
                kind_here, cluster = divmod(kind_row, cl_dev)
                base = kind_here * gc * tall + cluster * TILES
                wide_ref[pl.ds(base + t, gc, stride=tall), :] = summed[
                    kind_row * gc : (kind_row + 1) * gc, side * LANES : (side + 1) * LANES
                ]

    def narrow(pair, _):
        for which in range(2):
            start = (pair * 2 + which) * tall
            out_ref[pair, :, which * LANES : (which + 1) * LANES] = wide_ref[
                pl.ds(start, height), :
            ].astype(BF16)
        return 0

    lax.fori_loop(0, out_ref.shape[0], narrow, 0, unroll=4)


def own_operator_kernel(n_grp, n_row, cl_dev, cols_ref, rows_ref, live_ref, coupling_ref, *refs):
    out_ref, rest_ref, mine_ref, wide_ref, sems = refs
    per = coupling_ref.shape[0] // 3
    half = coupling_ref.shape[1] // 2
    copies = [
        pltpu.make_async_copy(
            coupling_ref.at[per : 2 * per, n * half : (n + 1) * half],
            mine_ref.at[:, n * half : (n + 1) * half],
            sems.at[n],
        )
        for n in range(2)
    ]
    others = [
        pltpu.make_async_copy(
            coupling_ref.at[2 * per * n : 2 * per * n + per],
            rest_ref.at[per * n : per * n + per],
            sems.at[2 + n],
        )
        for n in range(2)
    ]
    for copy in copies + others:
        copy.start()
    cut = slice(per, 2 * per)
    code = slot_codes(
        n_grp, n_row, cl_dev, 0, cols_ref[:, cut], rows_ref[:, cut], live_ref[:, cut]
    )

    def coupling_of(step):
        if step % (TILES // 4) == 0:
            copies[step // (TILES // 4)].wait()
        return mine_ref[:, step * 2 * LANES : (step + 1) * 2 * LANES]

    sum_slots(1, n_row * cl_dev, cl_dev, code, coupling_of, out_ref, wide_ref)
    for copy in others:
        copy.wait()


def side_operator_kernel(n_grp, n_row, cl_dev, cols_ref, rows_ref, live_ref, rest_ref, *refs):
    out_ref, wide_ref = refs
    per = rest_ref.shape[0] // 2

    def outer(ref):
        return jnp.concatenate([ref[:, :per], ref[:, 2 * per :]], axis=1)

    code = slot_codes(
        n_grp, n_row, cl_dev, 1, outer(cols_ref), outer(rows_ref), outer(live_ref)
    )

    def coupling_of(step):
        return rest_ref[:, step * 2 * LANES : (step + 1) * 2 * LANES]

    sum_slots(2, n_row * cl_dev, cl_dev, code, coupling_of, out_ref, wide_ref)


def far_pieces(total, pieces, pairs_piece):
    lane = lax.broadcasted_iota(jnp.int32, (K, LANES), 1)
    first = lane < K
    for operator_ref, base, piece_ref, places in pieces:
        for at, place in enumerate(places):
            for pair in range(pairs_piece):
                both = piece_ref[pl.ds((at * pairs_piece + pair) * K, K), :]
                swapped = jnp.concatenate([both[:, K:], both[:, :K]], axis=1)
                zero = jnp.zeros_like(both)
                weights = jnp.concatenate(
                    [
                        jnp.where(first, both, zero),
                        jnp.where(first, zero, swapped),
                        jnp.where(first, swapped, zero),
                        jnp.where(first, zero, both),
                    ],
                    axis=0,
                )
                index = base + place * pairs_piece + pair
                total = total + jnp.dot(
                    operator_ref[index], weights, preferred_element_type=F32
                )
    return total


def far_kernel(plan, pairs_piece, started, *refs):
    out_ref = refs[-1]
    total = refs[-2][...] if started else jnp.zeros(out_ref.shape, F32)
    pieces = [(refs[o], base, refs[p], places) for o, base, p, places in plan]
    out_ref[...] = far_pieces(total, pieces, pairs_piece)


def near_kernel(signal_ref, near_ref, basis_ref, total_ref, spread_ref):
    cl_dev = signal_ref.shape[0]
    for c in range(cl_dev):
        total = dot_nt(signal_ref[c], near_ref[c, 1])
        if c > 0:
            total = total + dot_nt(signal_ref[c - 1], near_ref[c, 0])
        if c < cl_dev - 1:
            total = total + dot_nt(signal_ref[c + 1], near_ref[c, 2])
        total_ref[:, c * LANES : (c + 1) * LANES] = total
    spread_ref[...] = jnp.zeros_like(spread_ref)
    for c in range(cl_dev):
        wide = basis_ref[c].astype(F32).reshape(TILES, HALVES, LANES)
        for parity in range(HALVES):
            start = parity * cl_dev * TILES + c * TILES
            spread_ref[start : start + TILES, c * LANES : (c + 1) * LANES] = wide[:, parity].astype(BF16)


def halo_kernel(n_dev, across_ref, along_ref, near_ref, so_far_ref, total_ref):
    cl_dev = near_ref.shape[0]
    row = lax.axis_index("row")
    me = lax.axis_index("grp") * lax.axis_size("row") + row
    odd = (row & 1) == 1
    across = across_ref[...]
    along = along_ref[...]
    zero = jnp.zeros_like(across)
    low = jnp.where(me == 0, zero, jnp.where(odd, across, along))
    high = jnp.where(me == n_dev - 1, zero, jnp.where(odd, along, across))
    total_ref[...] = so_far_ref[...]
    total_ref[:, :LANES] += dot_nt(low, near_ref[0, 0])
    total_ref[:, (cl_dev - 1) * LANES :] += dot_nt(high, near_ref[cl_dev - 1, 2])


def final_kernel(plan, pairs_piece, *refs):
    far_ref, near_total_ref, spread_ref, out_ref = refs[-4:]
    pieces = [(refs[o], base, refs[p], places) for o, base, p, places in plan]
    total = far_pieces(far_ref[...], pieces, pairs_piece)
    turned = total.T.astype(BF16)
    lhs = jnp.concatenate([turned[p * R : (p + 1) * R] for p in range(HALVES)], axis=1)
    res = near_total_ref[...] + jnp.dot(lhs, spread_ref[...], preferred_element_type=F32)
    for c in range(out_ref.shape[0]):
        out_ref[c] = res[:, c * LANES : (c + 1) * LANES].astype(BF16)


def held(*values):
    return [pltpu.with_memory_space_constraint(v, pltpu.VMEM) for v in values]


def per_device(signal, leaf_basis, near_blocks, coupling, block_cols, block_rows, block_live):
    cl_dev = signal.shape[0]
    n_row = lax.axis_size("row")
    n_grp = lax.axis_size("grp")
    n_dev = n_row * n_grp
    gc = cl_dev * n_row
    pairs_piece = cl_dev // 2
    pairs_kind = gc // 2
    height = cl_dev * TILES

    def across_row(value, bit):
        return lax.ppermute(value, "row", [(i, i ^ bit) for i in range(n_row)])

    partners = [(i, i ^ 1) for i in range(n_grp)]
    others = [(i, (i + 1) % n_grp if i % 2 else (i - 1) % n_grp) for i in range(n_grp)]
    n_slots = coupling.shape[0]

    signal, leaf_basis, cols, rows, live, mine, for_across, for_along = call(
        skeleton_kernel,
        [(signal.shape, BF16), (leaf_basis.shape, BF16)]
        + [((1, n_slots), jnp.int32)] * 3
        + [((cl_dev // 2 * K, LANES), BF16), ((R, LANES), BF16), ((R, LANES), BF16)],
        signal,
        leaf_basis,
        block_cols[None],
        block_rows[None],
        block_live[None],
        in_hbm=range(5),
        scratch=[pltpu.SemaphoreType.DMA((5,))],
    )

    def wide(n_kinds):
        return (n_kinds * gc * (height + PAD), LANES)

    own_operator, rest = call(
        functools.partial(own_operator_kernel, n_grp, n_row, cl_dev),
        [
            ((pairs_kind, height, 2 * LANES), BF16),
            ((n_slots // 3 * 2, coupling.shape[1]), BF16),
        ],
        cols,
        rows,
        live,
        coupling,
        in_hbm=(3,),
        scratch=[
            pltpu.VMEM((n_slots // 3, coupling.shape[1]), BF16),
            pltpu.VMEM(wide(1), F32),
            pltpu.SemaphoreType.DMA((4,)),
        ],
        room=wide(1)[0] * LANES * 4 + n_slots // 3 * coupling.shape[1] * 2,
    )
    side_operator = call(
        functools.partial(side_operator_kernel, n_grp, n_row, cl_dev),
        [((2 * pairs_kind, height, 2 * LANES), BF16)],
        cols,
        rows,
        live,
        rest,
        scratch=[pltpu.VMEM(wide(2), F32)],
        room=wide(2)[0] * LANES * 4,
    )
    (near_blocks,) = held(near_blocks)
    near_total, spread = call(
        near_kernel,
        [((R, cl_dev * LANES), F32), ((HALVES * height, cl_dev * LANES), BF16)],
        signal,
        near_blocks,
        leaf_basis,
    )

    places = [0]
    panel = mine
    bit = n_row // 2
    while bit > 1:
        got = across_row(panel, bit)
        panel = jnp.concatenate([panel, got], axis=0)
        places = places + [p ^ bit for p in places]
        bit //= 2
    over_y = across_row(panel, 1)
    places_y = [p ^ 1 for p in places]
    other_a = lax.ppermute(panel, "grp", others)
    across = across_row(for_across, 1)
    pairs = [(i, i + 1) for i in range(1, n_dev - 1, 2)]
    along = lax.ppermute(for_along, ("grp", "row"), pairs + [(b, a) for a, b in pairs])
    own_far = call(
        functools.partial(far_kernel, [(0, 0, 1, places)], pairs_piece, False),
        [((height, LANES), F32)],
        own_operator,
        *held(panel),
    )
    other_b = lax.ppermute(over_y, "grp", others)
    partner = lax.ppermute(jnp.concatenate([panel, over_y], axis=0), "grp", partners)

    with_halo = call(
        functools.partial(halo_kernel, n_dev),
        [((R, cl_dev * LANES), F32)],
        *held(across, along),
        near_blocks,
        near_total,
    )
    plan = [(0, 0, 2, places_y), (1, pairs_kind, 3, places), (1, 0, 4, places + places_y)]
    far = call(
        functools.partial(far_kernel, plan, pairs_piece, True),
        [((height, LANES), F32)],
        own_operator,
        side_operator,
        *held(over_y, other_a, partner),
        own_far,
    )
    return pl.pallas_call(
        functools.partial(final_kernel, [(0, pairs_kind, 1, places_y)], pairs_piece),
        out_shape=jax.ShapeDtypeStruct(signal.shape, BF16),
        in_specs=[pl.BlockSpec(memory_space=pltpu.VMEM)] * 5,
        out_specs=pl.BlockSpec(memory_space=pltpu.VMEM),
        compiler_params=pltpu.CompilerParams(vmem_limit_bytes=4 << 20),
        name="final",
    )(side_operator, *held(other_b), far, with_halo, spread)


def solution(mesh):
    in_specs = (
        P(("grp", "row"), None, None),
        P(("grp", "row"), None, None),
        P(("grp", "row"), None, None, None),
        P(("grp", "row"), None),
        P(("grp", "row")),
        P(("grp", "row")),
        P(("grp", "row")),
    )
    out_specs = P(("grp", "row"), None, None)

    return jax.shard_map(
        per_device, mesh=mesh, in_specs=in_specs, out_specs=out_specs, check_vma=False
    )
```

```python
import functools

import jax
import jax.numpy as jnp
from jax import lax
from jax.experimental import pallas as pl
from jax.experimental.pallas import tpu as pltpu
from jax.sharding import PartitionSpec as P


K = 64
R = 64
LANES = 128
HALVES = LANES // K
TILES = K // HALVES
PAD = 4


F32 = jnp.float32
BF16 = jnp.bfloat16


def dot_nt(a, b):
    return lax.dot_general(a, b, (((1,), (1,)), ((), ())), preferred_element_type=F32)


def call(kernel, outs, *args, scratch=(), room=0, in_hbm=()):
    spec = pl.BlockSpec(memory_space=pltpu.VMEM)
    far_spec = pl.BlockSpec(memory_space=pltpu.HBM)
    single = len(outs) == 1
    shapes = [pltpu.VMEM(s, d) for s, d in outs]
    args = [
        pltpu.with_memory_space_constraint(a, pltpu.HBM) if i in in_hbm else a
        for i, a in enumerate(args)
    ]
    return pl.pallas_call(
        kernel,
        out_shape=shapes[0] if single else shapes,
        in_specs=[far_spec if i in in_hbm else spec for i in range(len(args))],
        out_specs=spec if single else [spec] * len(outs),
        scratch_shapes=scratch,
        compiler_params=pltpu.CompilerParams(vmem_limit_bytes=room + (2 << 20)),
    )(*args)


def skeleton_kernel(*refs):
    sources, here, (out_ref, across_ref, along_ref, sems) = refs[:5], refs[5:10], refs[10:]
    copies = [pltpu.make_async_copy(a, b, sems.at[n]) for n, (a, b) in enumerate(zip(sources, here))]
    for copy in copies:
        copy.start()
    signal_ref, basis_ref = here[:2]
    copies[0].wait()
    copies[1].wait()
    last = signal_ref.shape[0] - 1
    for pair in range(signal_ref.shape[0] // 2):
        sides = [
            dot_nt(basis_ref[2 * pair + w], signal_ref[2 * pair + w]).astype(BF16) for w in range(2)
        ]
        out_ref[pl.ds(pair * K, K), :] = jnp.concatenate(sides, axis=1)
    odd = (lax.axis_index("row") & 1) == 1
    across_ref[...] = jnp.where(odd, signal_ref[0], signal_ref[last])
    along_ref[...] = jnp.where(odd, signal_ref[last], signal_ref[0])
    for copy in copies[2:]:
        copy.wait()


def slot_codes(n_grp, n_row, cl_dev, first_kind, cols, rows, live):
    gc = n_row * cl_dev
    shift = gc.bit_length() - 1
    local = cl_dev.bit_length() - 1
    group = lax.axis_index("grp")
    row = lax.axis_index("row")
    delta = (lax.shift_right_logical(cols, shift) - group + n_grp) & (n_grp - 1)
    partner = jnp.where((group & 1) == 0, 1, n_grp - 1)
    kind = jnp.where(delta == 0, 0, jnp.where(delta == partner, 1, 2)) - first_kind
    place = (cols & (gc - 1)) ^ lax.shift_left(row, local)
    return jnp.where(live > 0, kind * (cl_dev * gc) + rows * gc + place, -1)


def sum_slots(n_kinds, gc, cl_dev, code, coupling_of, out_ref, wide_ref):
    n_codes = n_kinds * cl_dev * gc
    shape = (n_codes, code.shape[1])
    select = (lax.broadcasted_iota(jnp.int32, shape, 0) == code).astype(F32).astype(BF16)
    height = cl_dev * TILES
    tall = height + PAD
    for step in range(TILES // 2):
        summed = jnp.dot(select, coupling_of(step), preferred_element_type=F32)
        for side in range(2):
            t = step * 2 + side
            for kind_row in range(n_kinds * cl_dev):
                kind_here, cluster = divmod(kind_row, cl_dev)
                base = kind_here * gc * tall + cluster * TILES
                wide_ref[pl.ds(base + t, gc, stride=tall), :] = summed[
                    kind_row * gc : (kind_row + 1) * gc, side * LANES : (side + 1) * LANES
                ]

    def narrow(pair, _):
        for which in range(2):
            start = (pair * 2 + which) * tall
            out_ref[pair, :, which * LANES : (which + 1) * LANES] = wide_ref[
                pl.ds(start, height), :
            ].astype(BF16)
        return 0

    lax.fori_loop(0, out_ref.shape[0], narrow, 0, unroll=4)


def own_operator_kernel(n_grp, n_row, cl_dev, cols_ref, rows_ref, live_ref, coupling_ref, *refs):
    out_ref, rest_ref, mine_ref, wide_ref, sems = refs
    per = coupling_ref.shape[0] // 3
    half = coupling_ref.shape[1] // 2
    copies = [
        pltpu.make_async_copy(
            coupling_ref.at[per : 2 * per, n * half : (n + 1) * half],
            mine_ref.at[:, n * half : (n + 1) * half],
            sems.at[n],
        )
        for n in range(2)
    ]
    others = [
        pltpu.make_async_copy(
            coupling_ref.at[2 * per * n : 2 * per * n + per],
            rest_ref.at[per * n : per * n + per],
            sems.at[2 + n],
        )
        for n in range(2)
    ]
    for copy in copies + others:
        copy.start()
    cut = slice(per, 2 * per)
    code = slot_codes(
        n_grp, n_row, cl_dev, 0, cols_ref[:, cut], rows_ref[:, cut], live_ref[:, cut]
    )

    def coupling_of(step):
        if step % (TILES // 4) == 0:
            copies[step // (TILES // 4)].wait()
        return mine_ref[:, step * 2 * LANES : (step + 1) * 2 * LANES]

    sum_slots(1, n_row * cl_dev, cl_dev, code, coupling_of, out_ref, wide_ref)
    for copy in others:
        copy.wait()


def side_operator_kernel(n_grp, n_row, cl_dev, cols_ref, rows_ref, live_ref, rest_ref, *refs):
    out_ref, wide_ref = refs
    per = rest_ref.shape[0] // 2

    def outer(ref):
        return jnp.concatenate([ref[:, :per], ref[:, 2 * per :]], axis=1)

    code = slot_codes(
        n_grp, n_row, cl_dev, 1, outer(cols_ref), outer(rows_ref), outer(live_ref)
    )

    def coupling_of(step):
        return rest_ref[:, step * 2 * LANES : (step + 1) * 2 * LANES]

    sum_slots(2, n_row * cl_dev, cl_dev, code, coupling_of, out_ref, wide_ref)


def far_pieces(total, pieces, pairs_piece):
    lane = lax.broadcasted_iota(jnp.int32, (K, LANES), 1)
    first = lane < K
    for operator_ref, base, piece_ref, places in pieces:
        for at, place in enumerate(places):
            for pair in range(pairs_piece):
                both = piece_ref[pl.ds((at * pairs_piece + pair) * K, K), :]
                swapped = jnp.concatenate([both[:, K:], both[:, :K]], axis=1)
                zero = jnp.zeros_like(both)
                weights = jnp.concatenate(
                    [
                        jnp.where(first, both, zero),
                        jnp.where(first, zero, swapped),
                        jnp.where(first, swapped, zero),
                        jnp.where(first, zero, both),
                    ],
                    axis=0,
                )
                index = base + place * pairs_piece + pair
                total = total + jnp.dot(
                    operator_ref[index], weights, preferred_element_type=F32
                )
    return total


def far_kernel(plan, pairs_piece, started, *refs):
    out_ref = refs[-1]
    total = refs[-2][...] if started else jnp.zeros(out_ref.shape, F32)
    pieces = [(refs[o], base, refs[p], places) for o, base, p, places in plan]
    out_ref[...] = far_pieces(total, pieces, pairs_piece)


def near_kernel(signal_ref, near_ref, basis_ref, total_ref, spread_ref):
    cl_dev = signal_ref.shape[0]
    for c in range(cl_dev):
        total = dot_nt(signal_ref[c], near_ref[c, 1])
        if c > 0:
            total = total + dot_nt(signal_ref[c - 1], near_ref[c, 0])
        if c < cl_dev - 1:
            total = total + dot_nt(signal_ref[c + 1], near_ref[c, 2])
        total_ref[:, c * LANES : (c + 1) * LANES] = total
    spread_ref[...] = jnp.zeros_like(spread_ref)
    for c in range(cl_dev):
        wide = basis_ref[c].astype(F32).reshape(TILES, HALVES, LANES)
        for parity in range(HALVES):
            start = parity * cl_dev * TILES + c * TILES
            spread_ref[start : start + TILES, c * LANES : (c + 1) * LANES] = wide[:, parity].astype(BF16)


def final_kernel(plan, pairs_piece, n_row, n_grp, *refs):
    other_ref, partner_ref, along_ref, across_ref, near_ref = refs[1:6]
    far_ref, near_total_ref, spread_ref, out_ref = refs[-4:]
    cl_dev = out_ref.shape[0]
    row = lax.axis_index("row")
    group = lax.axis_index("grp")
    odd = (row & 1) == 1
    odd_group = (group & 1) == 1
    from_other = other_ref[other_ref.shape[0] - R :]
    from_partner = partner_ref[partner_ref.shape[0] - R :]
    before = jnp.where(odd_group, from_partner, from_other)
    behind = jnp.where(odd_group, from_other, from_partner)
    along = jnp.where(row == 0, before, jnp.where(row == n_row - 1, behind, along_ref[...]))
    across = across_ref[...]
    zero = jnp.zeros_like(across)
    is_first = (row == 0) & (group == 0)
    is_last = (row == n_row - 1) & (group == n_grp - 1)
    low = jnp.where(is_first, zero, jnp.where(odd, across, along))
    high = jnp.where(is_last, zero, jnp.where(odd, along, across))
    sides = {0: dot_nt(low, near_ref[0, 0])}
    last = cl_dev - 1
    sides[last] = dot_nt(high, near_ref[last, 2])
    pieces = [(refs[o], base, refs[p], places) for o, base, p, places in plan]
    total = far_pieces(far_ref[...], pieces, pairs_piece)
    turned = total.T.astype(BF16)
    lhs = jnp.concatenate([turned[p * R : (p + 1) * R] for p in range(HALVES)], axis=1)
    res = near_total_ref[...] + jnp.dot(lhs, spread_ref[...], preferred_element_type=F32)
    for c in range(cl_dev):
        here = res[:, c * LANES : (c + 1) * LANES]
        if c in sides:
            here = here + sides[c]
        out_ref[c] = here.astype(BF16)


def held(*values):
    return [pltpu.with_memory_space_constraint(v, pltpu.VMEM) for v in values]


def per_device(signal, leaf_basis, near_blocks, coupling, block_cols, block_rows, block_live):
    cl_dev = signal.shape[0]
    n_row = lax.axis_size("row")
    n_grp = lax.axis_size("grp")
    gc = cl_dev * n_row
    pairs_piece = cl_dev // 2
    pairs_kind = gc // 2
    height = cl_dev * TILES

    def across_row(value, bit):
        return lax.ppermute(value, "row", [(i, i ^ bit) for i in range(n_row)])

    partners = [(i, i ^ 1) for i in range(n_grp)]
    others = [(i, (i + 1) % n_grp if i % 2 else (i - 1) % n_grp) for i in range(n_grp)]
    n_slots = coupling.shape[0]

    signal, leaf_basis, cols, rows, live, mine, for_across, for_along = call(
        skeleton_kernel,
        [(signal.shape, BF16), (leaf_basis.shape, BF16)]
        + [((1, n_slots), jnp.int32)] * 3
        + [((cl_dev // 2 * K, LANES), BF16), ((R, LANES), BF16), ((R, LANES), BF16)],
        signal,
        leaf_basis,
        block_cols[None],
        block_rows[None],
        block_live[None],
        in_hbm=range(5),
        scratch=[pltpu.SemaphoreType.DMA((5,))],
    )

    def wide(n_kinds):
        return (n_kinds * gc * (height + PAD), LANES)

    own_operator, rest = call(
        functools.partial(own_operator_kernel, n_grp, n_row, cl_dev),
        [
            ((pairs_kind, height, 2 * LANES), BF16),
            ((n_slots // 3 * 2, coupling.shape[1]), BF16),
        ],
        cols,
        rows,
        live,
        coupling,
        in_hbm=(3,),
        scratch=[
            pltpu.VMEM((n_slots // 3, coupling.shape[1]), BF16),
            pltpu.VMEM(wide(1), F32),
            pltpu.SemaphoreType.DMA((4,)),
        ],
        room=wide(1)[0] * LANES * 4 + n_slots // 3 * coupling.shape[1] * 2,
    )
    side_operator = call(
        functools.partial(side_operator_kernel, n_grp, n_row, cl_dev),
        [((2 * pairs_kind, height, 2 * LANES), BF16)],
        cols,
        rows,
        live,
        rest,
        scratch=[pltpu.VMEM(wide(2), F32)],
        room=wide(2)[0] * LANES * 4,
    )
    (near_blocks,) = held(near_blocks)
    near_total, spread = call(
        near_kernel,
        [((R, cl_dev * LANES), F32), ((HALVES * height, cl_dev * LANES), BF16)],
        signal,
        near_blocks,
        leaf_basis,
    )

    row = lax.axis_index("row")

    def packed(*values):
        return jnp.concatenate(values, axis=0)

    places = [0]
    panel = mine
    along = for_along
    bit = n_row // 2
    while bit > 1:
        size = panel.shape[0]
        got = across_row(packed(panel, along), bit)
        panel = packed(panel, got[:size])
        crosses = (row % bit == 0) | (row % bit == bit - 1)
        along = jnp.where(crosses, got[size:], along)
        places = places + [p ^ bit for p in places]
        bit //= 2
    size = panel.shape[0]
    got = across_row(packed(panel, along, for_across), 1)
    over_y, along, across = got[:size], got[size : size + R], got[size + R :]
    places_y = [p ^ 1 for p in places]
    other_a = lax.ppermute(panel, "grp", others)
    own_far = call(
        functools.partial(far_kernel, [(0, 0, 1, places)], pairs_piece, False),
        [((height, LANES), F32)],
        own_operator,
        *held(panel),
    )
    other_b = lax.ppermute(packed(over_y, along), "grp", others)
    partner = lax.ppermute(packed(panel, over_y, along), "grp", partners)

    plan = [(0, 0, 2, places_y), (1, pairs_kind, 3, places), (1, 0, 4, places + places_y)]
    far = call(
        functools.partial(far_kernel, plan, pairs_piece, True),
        [((height, LANES), F32)],
        own_operator,
        side_operator,
        *held(over_y, other_a, partner),
        own_far,
    )
    return pl.pallas_call(
        functools.partial(
            final_kernel, [(0, pairs_kind, 1, places_y)], pairs_piece, n_row, n_grp
        ),
        out_shape=jax.ShapeDtypeStruct(signal.shape, BF16),
        in_specs=[pl.BlockSpec(memory_space=pltpu.VMEM)] * 9,
        out_specs=pl.BlockSpec(memory_space=pltpu.VMEM),
        compiler_params=pltpu.CompilerParams(vmem_limit_bytes=4 << 20),
        name="final",
    )(
        side_operator,
        *held(other_b, partner, along, across),
        near_blocks,
        far,
        near_total,
        spread,
    )


def solution(mesh):
    in_specs = (
        P(("grp", "row"), None, None),
        P(("grp", "row"), None, None),
        P(("grp", "row"), None, None, None),
        P(("grp", "row"), None),
        P(("grp", "row")),
        P(("grp", "row")),
        P(("grp", "row")),
    )
    out_specs = P(("grp", "row"), None, None)

    return jax.shard_map(
        per_device, mesh=mesh, in_specs=in_specs, out_specs=out_specs, check_vma=False
    )
```

```python
import functools

import jax
import jax.numpy as jnp
from jax import lax
from jax.experimental import pallas as pl
from jax.experimental.pallas import tpu as pltpu
from jax.sharding import PartitionSpec as P


K = 64
R = 64
LANES = 128
HALVES = LANES // K
TILES = K // HALVES
PAD = 4


F32 = jnp.float32
BF16 = jnp.bfloat16


def dot_nt(a, b):
    return lax.dot_general(a, b, (((1,), (1,)), ((), ())), preferred_element_type=F32)


def call(kernel, outs, *args, scratch=(), room=0, in_hbm=()):
    spec = pl.BlockSpec(memory_space=pltpu.VMEM)
    far_spec = pl.BlockSpec(memory_space=pltpu.HBM)
    single = len(outs) == 1
    shapes = [pltpu.VMEM(s, d) for s, d in outs]
    args = [
        pltpu.with_memory_space_constraint(a, pltpu.HBM) if i in in_hbm else a
        for i, a in enumerate(args)
    ]
    return pl.pallas_call(
        kernel,
        out_shape=shapes[0] if single else shapes,
        in_specs=[far_spec if i in in_hbm else spec for i in range(len(args))],
        out_specs=spec if single else [spec] * len(outs),
        scratch_shapes=scratch,
        compiler_params=pltpu.CompilerParams(vmem_limit_bytes=room + (2 << 20)),
    )(*args)


def skeleton_kernel(*refs):
    sources, here, (out_ref, across_ref, along_ref, sems) = refs[:5], refs[5:10], refs[10:]
    copies = [pltpu.make_async_copy(a, b, sems.at[n]) for n, (a, b) in enumerate(zip(sources, here))]
    for copy in copies:
        copy.start()
    signal_ref, basis_ref = here[:2]
    copies[0].wait()
    copies[1].wait()
    last = signal_ref.shape[0] - 1
    for pair in range(signal_ref.shape[0] // 2):
        sides = [
            dot_nt(basis_ref[2 * pair + w], signal_ref[2 * pair + w]).astype(BF16) for w in range(2)
        ]
        out_ref[pl.ds(pair * K, K), :] = jnp.concatenate(sides, axis=1)
    odd = (lax.axis_index("row") & 1) == 1
    across_ref[...] = jnp.where(odd, signal_ref[0], signal_ref[last])
    along_ref[...] = jnp.where(odd, signal_ref[last], signal_ref[0])
    for copy in copies[2:]:
        copy.wait()


def slot_codes(n_grp, n_row, cl_dev, first_kind, cols, rows, live):
    gc = n_row * cl_dev
    shift = gc.bit_length() - 1
    local = cl_dev.bit_length() - 1
    group = lax.axis_index("grp")
    row = lax.axis_index("row")
    delta = (lax.shift_right_logical(cols, shift) - group + n_grp) & (n_grp - 1)
    partner = jnp.where((group & 1) == 0, 1, n_grp - 1)
    kind = jnp.where(delta == 0, 0, jnp.where(delta == partner, 1, 2)) - first_kind
    place = (cols & (gc - 1)) ^ lax.shift_left(row, local)
    return jnp.where(live > 0, kind * (cl_dev * gc) + rows * gc + place, -1)


def sum_slots(n_kinds, gc, cl_dev, code, coupling_of, out_ref, wide_ref):
    n_codes = n_kinds * cl_dev * gc
    shape = (n_codes, code.shape[1])
    select = (lax.broadcasted_iota(jnp.int32, shape, 0) == code).astype(F32).astype(BF16)
    height = cl_dev * TILES
    tall = height + PAD
    for step in range(TILES // 2):
        summed = jnp.dot(select, coupling_of(step), preferred_element_type=F32)
        for side in range(2):
            t = step * 2 + side
            for kind_row in range(n_kinds * cl_dev):
                kind_here, cluster = divmod(kind_row, cl_dev)
                base = kind_here * gc * tall + cluster * TILES
                wide_ref[pl.ds(base + t, gc, stride=tall), :] = summed[
                    kind_row * gc : (kind_row + 1) * gc, side * LANES : (side + 1) * LANES
                ]

    def narrow(pair, _):
        for which in range(2):
            start = (pair * 2 + which) * tall
            out_ref[pair, :, which * LANES : (which + 1) * LANES] = wide_ref[
                pl.ds(start, height), :
            ].astype(BF16)
        return 0

    lax.fori_loop(0, out_ref.shape[0], narrow, 0, unroll=4)


def own_operator_kernel(n_grp, n_row, cl_dev, cols_ref, rows_ref, live_ref, coupling_ref, *refs):
    out_ref, rest_ref, mine_ref, wide_ref, sems = refs
    per = coupling_ref.shape[0] // 3
    half = coupling_ref.shape[1] // 2
    copies = [
        pltpu.make_async_copy(
            coupling_ref.at[per : 2 * per, n * half : (n + 1) * half],
            mine_ref.at[:, n * half : (n + 1) * half],
            sems.at[n],
        )
        for n in range(2)
    ]
    others = [
        pltpu.make_async_copy(
            coupling_ref.at[2 * per * n : 2 * per * n + per],
            rest_ref.at[per * n : per * n + per],
            sems.at[2 + n],
        )
        for n in range(2)
    ]
    for copy in copies + others:
        copy.start()
    cut = slice(per, 2 * per)
    code = slot_codes(
        n_grp, n_row, cl_dev, 0, cols_ref[:, cut], rows_ref[:, cut], live_ref[:, cut]
    )

    def coupling_of(step):
        if step % (TILES // 4) == 0:
            copies[step // (TILES // 4)].wait()
        return mine_ref[:, step * 2 * LANES : (step + 1) * 2 * LANES]

    sum_slots(1, n_row * cl_dev, cl_dev, code, coupling_of, out_ref, wide_ref)
    for copy in others:
        copy.wait()


def side_operator_kernel(n_grp, n_row, cl_dev, cols_ref, rows_ref, live_ref, rest_ref, *refs):
    out_ref, wide_ref = refs
    per = rest_ref.shape[0] // 2

    def outer(ref):
        return jnp.concatenate([ref[:, :per], ref[:, 2 * per :]], axis=1)

    code = slot_codes(
        n_grp, n_row, cl_dev, 1, outer(cols_ref), outer(rows_ref), outer(live_ref)
    )

    def coupling_of(step):
        return rest_ref[:, step * 2 * LANES : (step + 1) * 2 * LANES]

    sum_slots(2, n_row * cl_dev, cl_dev, code, coupling_of, out_ref, wide_ref)


def far_pieces(total, pieces, pairs_piece):
    lane = lax.broadcasted_iota(jnp.int32, (K, LANES), 1)
    first = lane < K
    for operator_ref, base, piece_ref, places in pieces:
        for at, place in enumerate(places):
            for pair in range(pairs_piece):
                both = piece_ref[pl.ds((at * pairs_piece + pair) * K, K), :]
                swapped = jnp.concatenate([both[:, K:], both[:, :K]], axis=1)
                zero = jnp.zeros_like(both)
                weights = jnp.concatenate(
                    [
                        jnp.where(first, both, zero),
                        jnp.where(first, zero, swapped),
                        jnp.where(first, swapped, zero),
                        jnp.where(first, zero, both),
                    ],
                    axis=0,
                )
                index = base + place * pairs_piece + pair
                total = total + jnp.dot(
                    operator_ref[index], weights, preferred_element_type=F32
                )
    return total


def far_kernel(plan, pairs_piece, started, *refs):
    out_ref = refs[-1]
    total = refs[-2][...] if started else jnp.zeros(out_ref.shape, F32)
    pieces = [(refs[o], base, refs[p], places) for o, base, p, places in plan]
    out_ref[...] = far_pieces(total, pieces, pairs_piece)


def near_kernel(signal_ref, near_ref, basis_ref, total_ref, spread_ref):
    cl_dev = signal_ref.shape[0]
    for c in range(cl_dev):
        total = dot_nt(signal_ref[c], near_ref[c, 1])
        if c > 0:
            total = total + dot_nt(signal_ref[c - 1], near_ref[c, 0])
        if c < cl_dev - 1:
            total = total + dot_nt(signal_ref[c + 1], near_ref[c, 2])
        total_ref[:, c * LANES : (c + 1) * LANES] = total
    spread_ref[...] = jnp.zeros_like(spread_ref)
    for c in range(cl_dev):
        wide = basis_ref[c].astype(F32).reshape(TILES, HALVES, LANES)
        for parity in range(HALVES):
            start = parity * cl_dev * TILES + c * TILES
            spread_ref[start : start + TILES, c * LANES : (c + 1) * LANES] = wide[:, parity].astype(BF16)


def final_kernel(plan, pairs_piece, n_row, n_grp, *refs):
    other_ref, partner_ref, along_ref, across_ref, near_ref = refs[1:6]
    far_ref, near_total_ref, spread_ref, out_ref = refs[-4:]
    cl_dev = out_ref.shape[0]
    row = lax.axis_index("row")
    group = lax.axis_index("grp")
    odd = (row & 1) == 1
    odd_group = (group & 1) == 1
    from_other = other_ref[other_ref.shape[0] - R :]
    from_partner = partner_ref[partner_ref.shape[0] - R :]
    before = jnp.where(odd_group, from_partner, from_other)
    behind = jnp.where(odd_group, from_other, from_partner)
    along = jnp.where(row == 0, before, jnp.where(row == n_row - 1, behind, along_ref[...]))
    across = across_ref[...]
    zero = jnp.zeros_like(across)
    is_first = (row == 0) & (group == 0)
    is_last = (row == n_row - 1) & (group == n_grp - 1)
    low = jnp.where(is_first, zero, jnp.where(odd, across, along))
    high = jnp.where(is_last, zero, jnp.where(odd, along, across))
    sides = {0: dot_nt(low, near_ref[0, 0])}
    last = cl_dev - 1
    sides[last] = dot_nt(high, near_ref[last, 2])
    pieces = [(refs[o], base, refs[p], places) for o, base, p, places in plan]
    total = far_pieces(far_ref[...], pieces, pairs_piece)
    turned = total.T.astype(BF16)
    lhs = jnp.concatenate([turned[p * R : (p + 1) * R] for p in range(HALVES)], axis=1)
    res = near_total_ref[...] + jnp.dot(lhs, spread_ref[...], preferred_element_type=F32)
    for c in range(cl_dev):
        here = res[:, c * LANES : (c + 1) * LANES]
        if c in sides:
            here = here + sides[c]
        out_ref[c] = here.astype(BF16)


def held(*values):
    return [pltpu.with_memory_space_constraint(v, pltpu.VMEM) for v in values]


def per_device(signal, leaf_basis, near_blocks, coupling, block_cols, block_rows, block_live):
    cl_dev = signal.shape[0]
    n_row = lax.axis_size("row")
    n_grp = lax.axis_size("grp")
    gc = cl_dev * n_row
    pairs_piece = cl_dev // 2
    pairs_kind = gc // 2
    height = cl_dev * TILES

    def across_row(value, bit):
        return lax.ppermute(value, "row", [(i, i ^ bit) for i in range(n_row)])

    partners = [(i, i ^ 1) for i in range(n_grp)]
    others = [(i, (i + 1) % n_grp if i % 2 else (i - 1) % n_grp) for i in range(n_grp)]
    n_slots = coupling.shape[0]

    signal, leaf_basis, cols, rows, live, mine, for_across, for_along = call(
        skeleton_kernel,
        [(signal.shape, BF16), (leaf_basis.shape, BF16)]
        + [((1, n_slots), jnp.int32)] * 3
        + [((cl_dev // 2 * K, LANES), BF16), ((R, LANES), BF16), ((R, LANES), BF16)],
        signal,
        leaf_basis,
        block_cols[None],
        block_rows[None],
        block_live[None],
        in_hbm=range(5),
        scratch=[pltpu.SemaphoreType.DMA((5,))],
    )

    def wide(n_kinds):
        return (n_kinds * gc * (height + PAD), LANES)

    own_operator, rest = call(
        functools.partial(own_operator_kernel, n_grp, n_row, cl_dev),
        [
            ((pairs_kind, height, 2 * LANES), BF16),
            ((n_slots // 3 * 2, coupling.shape[1]), BF16),
        ],
        cols,
        rows,
        live,
        coupling,
        in_hbm=(3,),
        scratch=[
            pltpu.VMEM((n_slots // 3, coupling.shape[1]), BF16),
            pltpu.VMEM(wide(1), F32),
            pltpu.SemaphoreType.DMA((4,)),
        ],
        room=wide(1)[0] * LANES * 4 + n_slots // 3 * coupling.shape[1] * 2,
    )
    side_operator = call(
        functools.partial(side_operator_kernel, n_grp, n_row, cl_dev),
        [((2 * pairs_kind, height, 2 * LANES), BF16)],
        cols,
        rows,
        live,
        rest,
        scratch=[pltpu.VMEM(wide(2), F32)],
        room=wide(2)[0] * LANES * 4,
    )
    (near_blocks,) = held(near_blocks)
    near_total, spread = call(
        near_kernel,
        [((R, cl_dev * LANES), F32), ((HALVES * height, cl_dev * LANES), BF16)],
        signal,
        near_blocks,
        leaf_basis,
    )

    row = lax.axis_index("row")

    def packed(*values):
        return jnp.concatenate(values, axis=0)

    row = lax.axis_index("row")

    def packed(*values):
        return jnp.concatenate(values, axis=0)

    places = [0]
    panel = mine
    along = for_along
    bit = n_row // 2
    over_ya = None
    while bit > 1:
        size = panel.shape[0]
        got = across_row(packed(panel, along), bit)
        if bit == 2:
            over_ya = across_row(panel, 1)
            other_a = lax.ppermute(panel, "grp", others)
        panel = packed(panel, got[:size])
        crosses = (row % bit == 0) | (row % bit == bit - 1)
        along = jnp.where(crosses, got[size:], along)
        places = places + [p ^ bit for p in places]
        bit //= 2
    size = panel.shape[0] // 2
    places_y = [p ^ 1 for p in places]
    half = len(places) // 2
    got = across_row(packed(panel[size:], along, for_across), 1)
    leaps = [
        (g * n_row + r, h * n_row + (r ^ 1)) for g, h in others for r in range(n_row)
    ]
    other_b = lax.ppermute(packed(panel[size:], along), ("grp", "row"), leaps)
    over_yb, along, across = got[:size], got[size : size + R], got[size + R :]
    early_part = packed(panel, over_ya)
    early_places = places + places_y[:half]
    late_places = places_y[half:]
    other_c = lax.ppermute(packed(panel[size:], over_ya), "grp", others)
    own_far = call(
        functools.partial(far_kernel, [(0, 0, 1, early_places)], pairs_piece, False),
        [((height, LANES), F32)],
        own_operator,
        *held(early_part),
    )
    partner = lax.ppermute(packed(early_part, over_yb, along), "grp", partners)

    plan = [
        (0, 0, 2, late_places),
        (1, pairs_kind, 3, places[:half]),
        (1, 0, 4, early_places + late_places),
        (1, pairs_kind, 5, places[half:] + places_y[:half]),
    ]
    far = call(
        functools.partial(far_kernel, plan, pairs_piece, True),
        [((height, LANES), F32)],
        own_operator,
        side_operator,
        *held(over_yb, other_a, partner, other_c),
        own_far,
    )
    return pl.pallas_call(
        functools.partial(
            final_kernel, [(0, pairs_kind, 1, late_places)], pairs_piece, n_row, n_grp
        ),
        out_shape=jax.ShapeDtypeStruct(signal.shape, BF16),
        in_specs=[pl.BlockSpec(memory_space=pltpu.VMEM)] * 9,
        out_specs=pl.BlockSpec(memory_space=pltpu.VMEM),
        compiler_params=pltpu.CompilerParams(vmem_limit_bytes=4 << 20),
        name="final",
    )(
        side_operator,
        *held(other_b, partner, along, across),
        near_blocks,
        far,
        near_total,
        spread,
    )


def solution(mesh):
    in_specs = (
        P(("grp", "row"), None, None),
        P(("grp", "row"), None, None),
        P(("grp", "row"), None, None, None),
        P(("grp", "row"), None),
        P(("grp", "row")),
        P(("grp", "row")),
        P(("grp", "row")),
    )
    out_specs = P(("grp", "row"), None, None)

    return jax.shard_map(
        per_device, mesh=mesh, in_specs=in_specs, out_specs=out_specs, check_vma=False
    )
```

```python
import functools

import jax
import jax.numpy as jnp
from jax import lax
from jax.experimental import pallas as pl
from jax.experimental.pallas import tpu as pltpu
from jax.sharding import PartitionSpec as P


K = 64
R = 64
LANES = 128
HALVES = LANES // K
TILES = K // HALVES
PAD = 4


F32 = jnp.float32
BF16 = jnp.bfloat16


def dot_nt(a, b):
    return lax.dot_general(a, b, (((1,), (1,)), ((), ())), preferred_element_type=F32)


def call(kernel, outs, *args, scratch=(), room=0, in_hbm=()):
    spec = pl.BlockSpec(memory_space=pltpu.VMEM)
    far_spec = pl.BlockSpec(memory_space=pltpu.HBM)
    single = len(outs) == 1
    shapes = [pltpu.VMEM(s, d) for s, d in outs]
    args = [
        pltpu.with_memory_space_constraint(a, pltpu.HBM) if i in in_hbm else a
        for i, a in enumerate(args)
    ]
    return pl.pallas_call(
        kernel,
        out_shape=shapes[0] if single else shapes,
        in_specs=[far_spec if i in in_hbm else spec for i in range(len(args))],
        out_specs=spec if single else [spec] * len(outs),
        scratch_shapes=scratch,
        compiler_params=pltpu.CompilerParams(vmem_limit_bytes=room + (2 << 20)),
    )(*args)


def skeleton_kernel(*refs):
    sources, here, (out_ref, across_ref, along_ref, sems) = refs[:5], refs[5:10], refs[10:]
    copies = [pltpu.make_async_copy(a, b, sems.at[n]) for n, (a, b) in enumerate(zip(sources, here))]
    for copy in copies:
        copy.start()
    signal_ref, basis_ref = here[:2]
    copies[0].wait()
    copies[1].wait()
    last = signal_ref.shape[0] - 1
    for pair in range(signal_ref.shape[0] // 2):
        sides = [
            dot_nt(basis_ref[2 * pair + w], signal_ref[2 * pair + w]).astype(BF16) for w in range(2)
        ]
        out_ref[pl.ds(pair * K, K), :] = jnp.concatenate(sides, axis=1)
    odd = (lax.axis_index("row") & 1) == 1
    across_ref[...] = jnp.where(odd, signal_ref[0], signal_ref[last])
    along_ref[...] = jnp.where(odd, signal_ref[last], signal_ref[0])
    for copy in copies[2:]:
        copy.wait()


def slot_codes(n_grp, n_row, cl_dev, first_kind, cols, rows, live):
    gc = n_row * cl_dev
    shift = gc.bit_length() - 1
    local = cl_dev.bit_length() - 1
    group = lax.axis_index("grp")
    row = lax.axis_index("row")
    delta = (lax.shift_right_logical(cols, shift) - group + n_grp) & (n_grp - 1)
    partner = jnp.where((group & 1) == 0, 1, n_grp - 1)
    kind = jnp.where(delta == 0, 0, jnp.where(delta == partner, 1, 2)) - first_kind
    place = (cols & (gc - 1)) ^ lax.shift_left(row, local)
    return jnp.where(live > 0, kind * (cl_dev * gc) + rows * gc + place, -1)


def sum_slots(n_kinds, gc, cl_dev, code, coupling_of, out_ref, wide_ref):
    n_codes = n_kinds * cl_dev * gc
    shape = (n_codes, code.shape[1])
    select = (lax.broadcasted_iota(jnp.int32, shape, 0) == code).astype(F32).astype(BF16)
    height = cl_dev * TILES
    tall = height + PAD
    for step in range(TILES // 2):
        summed = jnp.dot(select, coupling_of(step), preferred_element_type=F32)
        for side in range(2):
            t = step * 2 + side
            for kind_row in range(n_kinds * cl_dev):
                kind_here, cluster = divmod(kind_row, cl_dev)
                base = kind_here * gc * tall + cluster * TILES
                wide_ref[pl.ds(base + t, gc, stride=tall), :] = summed[
                    kind_row * gc : (kind_row + 1) * gc, side * LANES : (side + 1) * LANES
                ]

    def narrow(pair, _):
        for which in range(2):
            start = (pair * 2 + which) * tall
            out_ref[pair, :, which * LANES : (which + 1) * LANES] = wide_ref[
                pl.ds(start, height), :
            ].astype(BF16)
        return 0

    lax.fori_loop(0, out_ref.shape[0], narrow, 0, unroll=4)


def own_operator_kernel(n_grp, n_row, cl_dev, cols_ref, rows_ref, live_ref, coupling_ref, *refs):
    out_ref, rest_ref, mine_ref, wide_ref, sems = refs
    per = coupling_ref.shape[0] // 3
    half = coupling_ref.shape[1] // 2
    copies = [
        pltpu.make_async_copy(
            coupling_ref.at[per : 2 * per, n * half : (n + 1) * half],
            mine_ref.at[:, n * half : (n + 1) * half],
            sems.at[n],
        )
        for n in range(2)
    ]
    others = [
        pltpu.make_async_copy(
            coupling_ref.at[2 * per * n : 2 * per * n + per],
            rest_ref.at[per * n : per * n + per],
            sems.at[2 + n],
        )
        for n in range(2)
    ]
    for copy in copies + others:
        copy.start()
    cut = slice(per, 2 * per)
    code = slot_codes(
        n_grp, n_row, cl_dev, 0, cols_ref[:, cut], rows_ref[:, cut], live_ref[:, cut]
    )

    def coupling_of(step):
        if step % (TILES // 4) == 0:
            copies[step // (TILES // 4)].wait()
        return mine_ref[:, step * 2 * LANES : (step + 1) * 2 * LANES]

    sum_slots(1, n_row * cl_dev, cl_dev, code, coupling_of, out_ref, wide_ref)
    for copy in others:
        copy.wait()


def side_operator_kernel(n_grp, n_row, cl_dev, cols_ref, rows_ref, live_ref, rest_ref, *refs):
    out_ref, wide_ref = refs
    per = rest_ref.shape[0] // 2

    def outer(ref):
        return jnp.concatenate([ref[:, :per], ref[:, 2 * per :]], axis=1)

    code = slot_codes(
        n_grp, n_row, cl_dev, 1, outer(cols_ref), outer(rows_ref), outer(live_ref)
    )

    def coupling_of(step):
        return rest_ref[:, step * 2 * LANES : (step + 1) * 2 * LANES]

    sum_slots(2, n_row * cl_dev, cl_dev, code, coupling_of, out_ref, wide_ref)


def far_pieces(total, pieces, pairs_piece):
    lane = lax.broadcasted_iota(jnp.int32, (K, LANES), 1)
    first = lane < K
    for operator_ref, base, piece_ref, places in pieces:
        for at, place in enumerate(places):
            for pair in range(pairs_piece):
                both = piece_ref[pl.ds((at * pairs_piece + pair) * K, K), :]
                swapped = jnp.concatenate([both[:, K:], both[:, :K]], axis=1)
                zero = jnp.zeros_like(both)
                weights = jnp.concatenate(
                    [
                        jnp.where(first, both, zero),
                        jnp.where(first, zero, swapped),
                        jnp.where(first, swapped, zero),
                        jnp.where(first, zero, both),
                    ],
                    axis=0,
                )
                index = base + place * pairs_piece + pair
                total = total + jnp.dot(
                    operator_ref[index], weights, preferred_element_type=F32
                )
    return total


def far_kernel(plan, pairs_piece, started, *refs):
    out_ref = refs[-1]
    total = refs[-2][...] if started else jnp.zeros(out_ref.shape, F32)
    pieces = [(refs[o], base, refs[p], places) for o, base, p, places in plan]
    out_ref[...] = far_pieces(total, pieces, pairs_piece)


def near_kernel(signal_ref, near_ref, basis_ref, total_ref, spread_ref):
    cl_dev = signal_ref.shape[0]
    for c in range(cl_dev):
        total = dot_nt(signal_ref[c], near_ref[c, 1])
        if c > 0:
            total = total + dot_nt(signal_ref[c - 1], near_ref[c, 0])
        if c < cl_dev - 1:
            total = total + dot_nt(signal_ref[c + 1], near_ref[c, 2])
        total_ref[:, c * LANES : (c + 1) * LANES] = total
    spread_ref[...] = jnp.zeros_like(spread_ref)
    for c in range(cl_dev):
        wide = basis_ref[c].astype(F32).reshape(TILES, HALVES, LANES)
        for parity in range(HALVES):
            start = parity * cl_dev * TILES + c * TILES
            spread_ref[start : start + TILES, c * LANES : (c + 1) * LANES] = wide[:, parity].astype(BF16)


def final_kernel(plan, pairs_piece, n_row, n_grp, *refs):
    other_ref, partner_ref, along_ref, across_ref, near_ref = refs[1:6]
    far_ref, near_total_ref, spread_ref, out_ref = refs[-4:]
    cl_dev = out_ref.shape[0]
    row = lax.axis_index("row")
    group = lax.axis_index("grp")
    odd = (row & 1) == 1
    odd_group = (group & 1) == 1
    from_other = other_ref[other_ref.shape[0] - R :]
    from_partner = partner_ref[partner_ref.shape[0] - R :]
    before = jnp.where(odd_group, from_partner, from_other)
    behind = jnp.where(odd_group, from_other, from_partner)
    along = jnp.where(row == 0, before, jnp.where(row == n_row - 1, behind, along_ref[...]))
    across = across_ref[...]
    zero = jnp.zeros_like(across)
    is_first = (row == 0) & (group == 0)
    is_last = (row == n_row - 1) & (group == n_grp - 1)
    low = jnp.where(is_first, zero, jnp.where(odd, across, along))
    high = jnp.where(is_last, zero, jnp.where(odd, along, across))
    sides = {0: dot_nt(low, near_ref[0, 0])}
    last = cl_dev - 1
    sides[last] = dot_nt(high, near_ref[last, 2])
    pieces = [(refs[o], base, refs[p], places) for o, base, p, places in plan]
    total = far_pieces(far_ref[...], pieces, pairs_piece)
    turned = total.T.astype(BF16)
    lhs = jnp.concatenate([turned[p * R : (p + 1) * R] for p in range(HALVES)], axis=1)
    res = near_total_ref[...] + jnp.dot(lhs, spread_ref[...], preferred_element_type=F32)
    for c in range(cl_dev):
        here = res[:, c * LANES : (c + 1) * LANES]
        if c in sides:
            here = here + sides[c]
        out_ref[c] = here.astype(BF16)


def held(*values):
    return [pltpu.with_memory_space_constraint(v, pltpu.VMEM) for v in values]


def per_device(signal, leaf_basis, near_blocks, coupling, block_cols, block_rows, block_live):
    cl_dev = signal.shape[0]
    n_row = lax.axis_size("row")
    n_grp = lax.axis_size("grp")
    gc = cl_dev * n_row
    pairs_piece = cl_dev // 2
    pairs_kind = gc // 2
    height = cl_dev * TILES

    def across_row(value, bit):
        return lax.ppermute(value, "row", [(i, i ^ bit) for i in range(n_row)])

    partners = [(i, i ^ 1) for i in range(n_grp)]
    others = [(i, (i + 1) % n_grp if i % 2 else (i - 1) % n_grp) for i in range(n_grp)]
    n_slots = coupling.shape[0]

    signal, leaf_basis, cols, rows, live, mine, for_across, for_along = call(
        skeleton_kernel,
        [(signal.shape, BF16), (leaf_basis.shape, BF16)]
        + [((1, n_slots), jnp.int32)] * 3
        + [((cl_dev // 2 * K, LANES), BF16), ((R, LANES), BF16), ((R, LANES), BF16)],
        signal,
        leaf_basis,
        block_cols[None],
        block_rows[None],
        block_live[None],
        in_hbm=range(5),
        scratch=[pltpu.SemaphoreType.DMA((5,))],
    )

    def wide(n_kinds):
        return (n_kinds * gc * (height + PAD), LANES)

    own_operator, rest = call(
        functools.partial(own_operator_kernel, n_grp, n_row, cl_dev),
        [
            ((pairs_kind, height, 2 * LANES), BF16),
            ((n_slots // 3 * 2, coupling.shape[1]), BF16),
        ],
        cols,
        rows,
        live,
        coupling,
        in_hbm=(3,),
        scratch=[
            pltpu.VMEM((n_slots // 3, coupling.shape[1]), BF16),
            pltpu.VMEM(wide(1), F32),
            pltpu.SemaphoreType.DMA((4,)),
        ],
        room=wide(1)[0] * LANES * 4 + n_slots // 3 * coupling.shape[1] * 2,
    )
    side_operator = call(
        functools.partial(side_operator_kernel, n_grp, n_row, cl_dev),
        [((2 * pairs_kind, height, 2 * LANES), BF16)],
        cols,
        rows,
        live,
        rest,
        scratch=[pltpu.VMEM(wide(2), F32)],
        room=wide(2)[0] * LANES * 4,
    )
    (near_blocks,) = held(near_blocks)
    near_total, spread = call(
        near_kernel,
        [((R, cl_dev * LANES), F32), ((HALVES * height, cl_dev * LANES), BF16)],
        signal,
        near_blocks,
        leaf_basis,
    )

    row = lax.axis_index("row")

    def packed(*values):
        return jnp.concatenate(values, axis=0)

    row = lax.axis_index("row")

    def packed(*values):
        return jnp.concatenate(values, axis=0)

    places = [0]
    panel = mine
    along = for_along
    bit = n_row // 2
    while bit > 4:
        size = panel.shape[0]
        got = across_row(packed(panel, along), bit)
        panel = packed(panel, got[:size])
        crosses = (row % bit == 0) | (row % bit == bit - 1)
        along = jnp.where(crosses, got[size:], along)
        places = places + [p ^ bit for p in places]
        bit //= 2
    size = panel.shape[0]
    got = across_row(panel, 4)
    with_along = packed(panel, along)
    near_z = across_row(with_along, 2)
    far_z = across_row(with_along, 6)
    places = places + [p ^ 4 for p in places]
    places = places + [p ^ 2 for p in places]
    first_half = packed(panel, got)
    over_ya = across_row(first_half, 1)
    other_a = lax.ppermute(first_half, "grp", others)
    panel = packed(first_half, near_z[:size], far_z[:size])
    along = jnp.where((row % 4 == 1) | (row % 4 == 2), far_z[size:], near_z[size:])
    size = panel.shape[0] // 2
    places_y = [p ^ 1 for p in places]
    half = len(places) // 2
    got = across_row(packed(panel[size:], along, for_across), 1)
    leaps = [
        (g * n_row + r, h * n_row + (r ^ 1)) for g, h in others for r in range(n_row)
    ]
    other_b = lax.ppermute(packed(panel[size:], along), ("grp", "row"), leaps)
    over_yb, along, across = got[:size], got[size : size + R], got[size + R :]
    early_part = packed(panel, over_ya)
    early_places = places + places_y[:half]
    late_places = places_y[half:]
    other_c = lax.ppermute(over_ya, "grp", others)
    other_e = across_row(other_a, 2)
    own_far = call(
        functools.partial(far_kernel, [(0, 0, 1, early_places)], pairs_piece, False),
        [((height, LANES), F32)],
        own_operator,
        *held(early_part),
    )
    partner = lax.ppermute(packed(early_part, over_yb, along), "grp", partners)

    plan = [
        (0, 0, 2, late_places),
        (1, pairs_kind, 3, places[:half]),
        (1, 0, 4, early_places + late_places),
        (1, pairs_kind, 5, places_y[:half]),
        (1, pairs_kind, 6, places[half:]),
    ]
    far = call(
        functools.partial(far_kernel, plan, pairs_piece, True),
        [((height, LANES), F32)],
        own_operator,
        side_operator,
        *held(over_yb, other_a, partner, other_c, other_e),
        own_far,
    )
    return pl.pallas_call(
        functools.partial(
            final_kernel, [(0, pairs_kind, 1, late_places)], pairs_piece, n_row, n_grp
        ),
        out_shape=jax.ShapeDtypeStruct(signal.shape, BF16),
        in_specs=[pl.BlockSpec(memory_space=pltpu.VMEM)] * 9,
        out_specs=pl.BlockSpec(memory_space=pltpu.VMEM),
        compiler_params=pltpu.CompilerParams(vmem_limit_bytes=4 << 20),
        name="final",
    )(
        side_operator,
        *held(other_b, partner, along, across),
        near_blocks,
        far,
        near_total,
        spread,
    )


def solution(mesh):
    in_specs = (
        P(("grp", "row"), None, None),
        P(("grp", "row"), None, None),
        P(("grp", "row"), None, None, None),
        P(("grp", "row"), None),
        P(("grp", "row")),
        P(("grp", "row")),
        P(("grp", "row")),
    )
    out_specs = P(("grp", "row"), None, None)

    return jax.shard_map(
        per_device, mesh=mesh, in_specs=in_specs, out_specs=out_specs, check_vma=False
    )
```

```python
import functools

import jax
import jax.numpy as jnp
from jax import lax
from jax.experimental import pallas as pl
from jax.experimental.pallas import tpu as pltpu
from jax.sharding import PartitionSpec as P


K = 64
R = 64
LANES = 128
HALVES = LANES // K
TILES = K // HALVES
PAD = 4


F32 = jnp.float32
BF16 = jnp.bfloat16


def dot_nt(a, b):
    return lax.dot_general(a, b, (((1,), (1,)), ((), ())), preferred_element_type=F32)


def call(kernel, outs, *args, scratch=(), room=0, in_hbm=()):
    spec = pl.BlockSpec(memory_space=pltpu.VMEM)
    far_spec = pl.BlockSpec(memory_space=pltpu.HBM)
    single = len(outs) == 1
    shapes = [pltpu.VMEM(s, d) for s, d in outs]
    args = [
        pltpu.with_memory_space_constraint(a, pltpu.HBM) if i in in_hbm else a
        for i, a in enumerate(args)
    ]
    return pl.pallas_call(
        kernel,
        out_shape=shapes[0] if single else shapes,
        in_specs=[far_spec if i in in_hbm else spec for i in range(len(args))],
        out_specs=spec if single else [spec] * len(outs),
        scratch_shapes=scratch,
        compiler_params=pltpu.CompilerParams(vmem_limit_bytes=room + (2 << 20)),
    )(*args)


def skeleton_kernel(*refs):
    sources, here, (out_ref, across_ref, along_ref, sems) = refs[:5], refs[5:10], refs[10:]
    copies = [pltpu.make_async_copy(a, b, sems.at[n]) for n, (a, b) in enumerate(zip(sources, here))]
    for copy in copies:
        copy.start()
    signal_ref, basis_ref = here[:2]
    copies[0].wait()
    copies[1].wait()
    last = signal_ref.shape[0] - 1
    for pair in range(signal_ref.shape[0] // 2):
        sides = [
            dot_nt(basis_ref[2 * pair + w], signal_ref[2 * pair + w]).astype(BF16) for w in range(2)
        ]
        out_ref[pl.ds(pair * K, K), :] = jnp.concatenate(sides, axis=1)
    odd = (lax.axis_index("row") & 1) == 1
    across_ref[...] = jnp.where(odd, signal_ref[0], signal_ref[last])
    along_ref[...] = jnp.where(odd, signal_ref[last], signal_ref[0])
    for copy in copies[2:]:
        copy.wait()


def slot_codes(n_grp, n_row, cl_dev, first_kind, cols, rows, live):
    gc = n_row * cl_dev
    shift = gc.bit_length() - 1
    local = cl_dev.bit_length() - 1
    group = lax.axis_index("grp")
    row = lax.axis_index("row")
    delta = (lax.shift_right_logical(cols, shift) - group + n_grp) & (n_grp - 1)
    partner = jnp.where((group & 1) == 0, 1, n_grp - 1)
    kind = jnp.where(delta == 0, 0, jnp.where(delta == partner, 1, 2)) - first_kind
    place = (cols & (gc - 1)) ^ lax.shift_left(row, local)
    return jnp.where(live > 0, kind * (cl_dev * gc) + rows * gc + place, -1)


def sum_slots(n_kinds, gc, cl_dev, code, coupling_of, out_ref, wide_ref):
    n_codes = n_kinds * cl_dev * gc
    shape = (n_codes, code.shape[1])
    select = (lax.broadcasted_iota(jnp.int32, shape, 0) == code).astype(F32).astype(BF16)
    height = cl_dev * TILES
    tall = height + PAD
    for step in range(TILES // 2):
        summed = jnp.dot(select, coupling_of(step), preferred_element_type=F32)
        for side in range(2):
            t = step * 2 + side
            for kind_row in range(n_kinds * cl_dev):
                kind_here, cluster = divmod(kind_row, cl_dev)
                base = kind_here * gc * tall + cluster * TILES
                wide_ref[pl.ds(base + t, gc, stride=tall), :] = summed[
                    kind_row * gc : (kind_row + 1) * gc, side * LANES : (side + 1) * LANES
                ]

    def narrow(pair, _):
        for which in range(2):
            start = (pair * 2 + which) * tall
            out_ref[pair, :, which * LANES : (which + 1) * LANES] = wide_ref[
                pl.ds(start, height), :
            ].astype(BF16)
        return 0

    lax.fori_loop(0, out_ref.shape[0], narrow, 0, unroll=4)


def own_operator_kernel(n_grp, n_row, cl_dev, cols_ref, rows_ref, live_ref, coupling_ref, *refs):
    out_ref, rest_ref, mine_ref, wide_ref, sems = refs
    per = coupling_ref.shape[0] // 3
    half = coupling_ref.shape[1] // 2
    copies = [
        pltpu.make_async_copy(
            coupling_ref.at[per : 2 * per, n * half : (n + 1) * half],
            mine_ref.at[:, n * half : (n + 1) * half],
            sems.at[n],
        )
        for n in range(2)
    ]
    others = [
        pltpu.make_async_copy(
            coupling_ref.at[2 * per * n : 2 * per * n + per],
            rest_ref.at[per * n : per * n + per],
            sems.at[2 + n],
        )
        for n in range(2)
    ]
    for copy in copies + others:
        copy.start()
    cut = slice(per, 2 * per)
    code = slot_codes(
        n_grp, n_row, cl_dev, 0, cols_ref[:, cut], rows_ref[:, cut], live_ref[:, cut]
    )

    def coupling_of(step):
        if step % (TILES // 4) == 0:
            copies[step // (TILES // 4)].wait()
        return mine_ref[:, step * 2 * LANES : (step + 1) * 2 * LANES]

    sum_slots(1, n_row * cl_dev, cl_dev, code, coupling_of, out_ref, wide_ref)
    for copy in others:
        copy.wait()


def side_operator_kernel(n_grp, n_row, cl_dev, cols_ref, rows_ref, live_ref, rest_ref, *refs):
    out_ref, wide_ref = refs
    per = rest_ref.shape[0] // 2

    def outer(ref):
        return jnp.concatenate([ref[:, :per], ref[:, 2 * per :]], axis=1)

    code = slot_codes(
        n_grp, n_row, cl_dev, 1, outer(cols_ref), outer(rows_ref), outer(live_ref)
    )

    def coupling_of(step):
        return rest_ref[:, step * 2 * LANES : (step + 1) * 2 * LANES]

    sum_slots(2, n_row * cl_dev, cl_dev, code, coupling_of, out_ref, wide_ref)


def far_pieces(total, pieces, pairs_piece):
    lane = lax.broadcasted_iota(jnp.int32, (K, LANES), 1)
    first = lane < K
    for operator_ref, base, piece_ref, places in pieces:
        for at, place in enumerate(places):
            for pair in range(pairs_piece):
                both = piece_ref[pl.ds((at * pairs_piece + pair) * K, K), :]
                swapped = jnp.concatenate([both[:, K:], both[:, :K]], axis=1)
                zero = jnp.zeros_like(both)
                weights = jnp.concatenate(
                    [
                        jnp.where(first, both, zero),
                        jnp.where(first, zero, swapped),
                        jnp.where(first, swapped, zero),
                        jnp.where(first, zero, both),
                    ],
                    axis=0,
                )
                index = base + place * pairs_piece + pair
                total = total + jnp.dot(
                    operator_ref[index], weights, preferred_element_type=F32
                )
    return total


def far_kernel(plan, pairs_piece, started, *refs):
    out_ref = refs[-1]
    total = refs[-2][...] if started else jnp.zeros(out_ref.shape, F32)
    pieces = [(refs[o], base, refs[p], places) for o, base, p, places in plan]
    out_ref[...] = far_pieces(total, pieces, pairs_piece)


def near_kernel(signal_ref, near_ref, basis_ref, total_ref, spread_ref):
    cl_dev = signal_ref.shape[0]
    for c in range(cl_dev):
        total = dot_nt(signal_ref[c], near_ref[c, 1])
        if c > 0:
            total = total + dot_nt(signal_ref[c - 1], near_ref[c, 0])
        if c < cl_dev - 1:
            total = total + dot_nt(signal_ref[c + 1], near_ref[c, 2])
        total_ref[:, c * LANES : (c + 1) * LANES] = total
    spread_ref[...] = jnp.zeros_like(spread_ref)
    for c in range(cl_dev):
        wide = basis_ref[c].astype(F32).reshape(TILES, HALVES, LANES)
        for parity in range(HALVES):
            start = parity * cl_dev * TILES + c * TILES
            spread_ref[start : start + TILES, c * LANES : (c + 1) * LANES] = wide[:, parity].astype(BF16)


def final_kernel(plan, pairs_piece, n_row, n_grp, *refs):
    other_ref, partner_ref, along_ref, across_ref, near_ref = refs[1:6]
    far_ref, near_total_ref, spread_ref, out_ref = refs[-4:]
    cl_dev = out_ref.shape[0]
    row = lax.axis_index("row")
    group = lax.axis_index("grp")
    odd = (row & 1) == 1
    odd_group = (group & 1) == 1
    from_other = other_ref[other_ref.shape[0] - R :]
    from_partner = partner_ref[partner_ref.shape[0] - R :]
    before = jnp.where(odd_group, from_partner, from_other)
    behind = jnp.where(odd_group, from_other, from_partner)
    along = jnp.where(row == 0, before, jnp.where(row == n_row - 1, behind, along_ref[...]))
    across = across_ref[...]
    zero = jnp.zeros_like(across)
    is_first = (row == 0) & (group == 0)
    is_last = (row == n_row - 1) & (group == n_grp - 1)
    low = jnp.where(is_first, zero, jnp.where(odd, across, along))
    high = jnp.where(is_last, zero, jnp.where(odd, along, across))
    sides = {0: dot_nt(low, near_ref[0, 0])}
    last = cl_dev - 1
    sides[last] = dot_nt(high, near_ref[last, 2])
    pieces = [(refs[o], base, refs[p], places) for o, base, p, places in plan]
    total = far_pieces(far_ref[...], pieces, pairs_piece)
    turned = total.T.astype(BF16)
    lhs = jnp.concatenate([turned[p * R : (p + 1) * R] for p in range(HALVES)], axis=1)
    res = near_total_ref[...] + jnp.dot(lhs, spread_ref[...], preferred_element_type=F32)
    for c in range(cl_dev):
        here = res[:, c * LANES : (c + 1) * LANES]
        if c in sides:
            here = here + sides[c]
        out_ref[c] = here.astype(BF16)


def held(*values):
    return [pltpu.with_memory_space_constraint(v, pltpu.VMEM) for v in values]


def per_device(signal, leaf_basis, near_blocks, coupling, block_cols, block_rows, block_live):
    cl_dev = signal.shape[0]
    n_row = lax.axis_size("row")
    n_grp = lax.axis_size("grp")
    gc = cl_dev * n_row
    pairs_piece = cl_dev // 2
    pairs_kind = gc // 2
    height = cl_dev * TILES

    def across_row(value, bit):
        return lax.ppermute(value, "row", [(i, i ^ bit) for i in range(n_row)])

    partners = [(i, i ^ 1) for i in range(n_grp)]
    others = [(i, (i + 1) % n_grp if i % 2 else (i - 1) % n_grp) for i in range(n_grp)]
    n_slots = coupling.shape[0]

    signal, leaf_basis, cols, rows, live, mine, for_across, for_along = call(
        skeleton_kernel,
        [(signal.shape, BF16), (leaf_basis.shape, BF16)]
        + [((1, n_slots), jnp.int32)] * 3
        + [((cl_dev // 2 * K, LANES), BF16), ((R, LANES), BF16), ((R, LANES), BF16)],
        signal,
        leaf_basis,
        block_cols[None],
        block_rows[None],
        block_live[None],
        in_hbm=range(5),
        scratch=[pltpu.SemaphoreType.DMA((5,))],
    )

    def wide(n_kinds):
        return (n_kinds * gc * (height + PAD), LANES)

    own_operator, rest = call(
        functools.partial(own_operator_kernel, n_grp, n_row, cl_dev),
        [
            ((pairs_kind, height, 2 * LANES), BF16),
            ((n_slots // 3 * 2, coupling.shape[1]), BF16),
        ],
        cols,
        rows,
        live,
        coupling,
        in_hbm=(3,),
        scratch=[
            pltpu.VMEM((n_slots // 3, coupling.shape[1]), BF16),
            pltpu.VMEM(wide(1), F32),
            pltpu.SemaphoreType.DMA((4,)),
        ],
        room=wide(1)[0] * LANES * 4 + n_slots // 3 * coupling.shape[1] * 2,
    )
    side_operator = call(
        functools.partial(side_operator_kernel, n_grp, n_row, cl_dev),
        [((2 * pairs_kind, height, 2 * LANES), BF16)],
        cols,
        rows,
        live,
        rest,
        scratch=[pltpu.VMEM(wide(2), F32)],
        room=wide(2)[0] * LANES * 4,
    )
    (near_blocks,) = held(near_blocks)
    near_total, spread = call(
        near_kernel,
        [((R, cl_dev * LANES), F32), ((HALVES * height, cl_dev * LANES), BF16)],
        signal,
        near_blocks,
        leaf_basis,
    )

    row = lax.axis_index("row")

    def packed(*values):
        return jnp.concatenate(values, axis=0)

    row = lax.axis_index("row")

    def packed(*values):
        return jnp.concatenate(values, axis=0)

    places = [0]
    panel = mine
    along = for_along
    bit = n_row // 2
    while bit > 4:
        size = panel.shape[0]
        got = across_row(packed(panel, along), bit)
        panel = packed(panel, got[:size])
        crosses = (row % bit == 0) | (row % bit == bit - 1)
        along = jnp.where(crosses, got[size:], along)
        places = places + [p ^ bit for p in places]
        bit //= 2
    size = panel.shape[0]
    got = across_row(panel, 4)
    with_along = packed(panel, along)
    near_z = across_row(with_along, 2)
    far_z = across_row(with_along, 6)
    places = places + [p ^ 4 for p in places]
    places = places + [p ^ 2 for p in places]
    first_half = packed(panel, got)
    got = across_row(packed(first_half, for_across), 1)
    over_ya, across = got[: 2 * size], got[2 * size :]
    other_a = lax.ppermute(first_half, "grp", others)
    panel = packed(first_half, near_z[:size], far_z[:size])
    along = jnp.where((row % 4 == 1) | (row % 4 == 2), far_z[size:], near_z[size:])
    size = panel.shape[0] // 2
    places_y = [p ^ 1 for p in places]
    half = len(places) // 2
    got = across_row(packed(panel[size:], along), 1)
    leaps = [
        (g * n_row + r, h * n_row + (r ^ 1)) for g, h in others for r in range(n_row)
    ]
    other_b = lax.ppermute(packed(panel[size:], along), ("grp", "row"), leaps)
    over_yb, along = got[:size], got[size:]
    early_part = packed(panel, over_ya)
    early_places = places + places_y[:half]
    late_places = places_y[half:]
    other_c = lax.ppermute(over_ya, "grp", others)
    other_e = across_row(other_a, 2)
    own_far = call(
        functools.partial(far_kernel, [(0, 0, 1, early_places)], pairs_piece, False),
        [((height, LANES), F32)],
        own_operator,
        *held(early_part),
    )
    partner = lax.ppermute(packed(early_part, over_yb, along), "grp", partners)

    plan = [
        (0, 0, 2, late_places),
        (1, pairs_kind, 3, places[:half]),
        (1, 0, 4, early_places + late_places),
        (1, pairs_kind, 5, places_y[:half]),
        (1, pairs_kind, 6, places[half:]),
    ]
    far = call(
        functools.partial(far_kernel, plan, pairs_piece, True),
        [((height, LANES), F32)],
        own_operator,
        side_operator,
        *held(over_yb, other_a, partner, other_c, other_e),
        own_far,
    )
    return pl.pallas_call(
        functools.partial(
            final_kernel, [(0, pairs_kind, 1, late_places)], pairs_piece, n_row, n_grp
        ),
        out_shape=jax.ShapeDtypeStruct(signal.shape, BF16),
        in_specs=[pl.BlockSpec(memory_space=pltpu.VMEM)] * 9,
        out_specs=pl.BlockSpec(memory_space=pltpu.VMEM),
        compiler_params=pltpu.CompilerParams(vmem_limit_bytes=4 << 20),
        name="final",
    )(
        side_operator,
        *held(other_b, partner, along, across),
        near_blocks,
        far,
        near_total,
        spread,
    )


def solution(mesh):
    in_specs = (
        P(("grp", "row"), None, None),
        P(("grp", "row"), None, None),
        P(("grp", "row"), None, None, None),
        P(("grp", "row"), None),
        P(("grp", "row")),
        P(("grp", "row")),
        P(("grp", "row")),
    )
    out_specs = P(("grp", "row"), None, None)

    return jax.shard_map(
        per_device, mesh=mesh, in_specs=in_specs, out_specs=out_specs, check_vma=False
    )
```

```python
import functools

import jax
import jax.numpy as jnp
from jax import lax
from jax.experimental import pallas as pl
from jax.experimental.pallas import tpu as pltpu
from jax.sharding import PartitionSpec as P


K = 64
R = 64
LANES = 128
HALVES = LANES // K
TILES = K // HALVES
PAD = 4


F32 = jnp.float32
BF16 = jnp.bfloat16


def dot_nt(a, b):
    return lax.dot_general(a, b, (((1,), (1,)), ((), ())), preferred_element_type=F32)


def call(kernel, outs, *args, scratch=(), room=0, in_hbm=()):
    spec = pl.BlockSpec(memory_space=pltpu.VMEM)
    far_spec = pl.BlockSpec(memory_space=pltpu.HBM)
    single = len(outs) == 1
    shapes = [pltpu.VMEM(s, d) for s, d in outs]
    args = [
        pltpu.with_memory_space_constraint(a, pltpu.HBM) if i in in_hbm else a
        for i, a in enumerate(args)
    ]
    return pl.pallas_call(
        kernel,
        out_shape=shapes[0] if single else shapes,
        in_specs=[far_spec if i in in_hbm else spec for i in range(len(args))],
        out_specs=spec if single else [spec] * len(outs),
        scratch_shapes=scratch,
        compiler_params=pltpu.CompilerParams(vmem_limit_bytes=room + (2 << 20)),
    )(*args)


def skeleton_kernel(*refs):
    sources, here, (out_ref, across_ref, along_ref, sems) = refs[:5], refs[5:10], refs[10:]
    copies = [pltpu.make_async_copy(a, b, sems.at[n]) for n, (a, b) in enumerate(zip(sources, here))]
    for copy in copies:
        copy.start()
    signal_ref, basis_ref = here[:2]
    copies[0].wait()
    copies[1].wait()
    last = signal_ref.shape[0] - 1
    for pair in range(signal_ref.shape[0] // 2):
        sides = [
            dot_nt(basis_ref[2 * pair + w], signal_ref[2 * pair + w]).astype(BF16) for w in range(2)
        ]
        out_ref[pl.ds(pair * K, K), :] = jnp.concatenate(sides, axis=1)
    odd = (lax.axis_index("row") & 1) == 1
    across_ref[...] = jnp.where(odd, signal_ref[0], signal_ref[last])
    along_ref[...] = jnp.where(odd, signal_ref[last], signal_ref[0])
    for copy in copies[2:]:
        copy.wait()


def slot_codes(n_grp, n_row, cl_dev, first_kind, cols, rows, live):
    gc = n_row * cl_dev
    shift = gc.bit_length() - 1
    local = cl_dev.bit_length() - 1
    group = lax.axis_index("grp")
    row = lax.axis_index("row")
    delta = (lax.shift_right_logical(cols, shift) - group + n_grp) & (n_grp - 1)
    partner = jnp.where((group & 1) == 0, 1, n_grp - 1)
    kind = jnp.where(delta == 0, 0, jnp.where(delta == partner, 1, 2)) - first_kind
    place = (cols & (gc - 1)) ^ lax.shift_left(row, local)
    return jnp.where(live > 0, kind * (cl_dev * gc) + rows * gc + place, -1)


def sum_slots(n_kinds, gc, cl_dev, code, coupling_of, out_ref, wide_ref):
    n_codes = n_kinds * cl_dev * gc
    shape = (n_codes, code.shape[1])
    select = (lax.broadcasted_iota(jnp.int32, shape, 0) == code).astype(F32).astype(BF16)
    height = cl_dev * TILES
    tall = height + PAD
    for step in range(TILES // 2):
        summed = jnp.dot(select, coupling_of(step), preferred_element_type=F32)
        for side in range(2):
            t = step * 2 + side
            for kind_row in range(n_kinds * cl_dev):
                kind_here, cluster = divmod(kind_row, cl_dev)
                base = kind_here * gc * tall + cluster * TILES
                wide_ref[pl.ds(base + t, gc, stride=tall), :] = summed[
                    kind_row * gc : (kind_row + 1) * gc, side * LANES : (side + 1) * LANES
                ]

    def narrow(pair, _):
        for which in range(2):
            start = (pair * 2 + which) * tall
            out_ref[pair, :, which * LANES : (which + 1) * LANES] = wide_ref[
                pl.ds(start, height), :
            ].astype(BF16)
        return 0

    lax.fori_loop(0, out_ref.shape[0], narrow, 0, unroll=4)


def own_operator_kernel(n_grp, n_row, cl_dev, cols_ref, rows_ref, live_ref, coupling_ref, *refs):
    out_ref, rest_ref, mine_ref, wide_ref, sems = refs
    per = coupling_ref.shape[0] // 3
    half = coupling_ref.shape[1] // 2
    copies = [
        pltpu.make_async_copy(
            coupling_ref.at[per : 2 * per, n * half : (n + 1) * half],
            mine_ref.at[:, n * half : (n + 1) * half],
            sems.at[n],
        )
        for n in range(2)
    ]
    others = [
        pltpu.make_async_copy(
            coupling_ref.at[2 * per * n : 2 * per * n + per],
            rest_ref.at[per * n : per * n + per],
            sems.at[2 + n],
        )
        for n in range(2)
    ]
    for copy in copies + others:
        copy.start()
    cut = slice(per, 2 * per)
    code = slot_codes(
        n_grp, n_row, cl_dev, 0, cols_ref[:, cut], rows_ref[:, cut], live_ref[:, cut]
    )

    def coupling_of(step):
        if step % (TILES // 4) == 0:
            copies[step // (TILES // 4)].wait()
        return mine_ref[:, step * 2 * LANES : (step + 1) * 2 * LANES]

    sum_slots(1, n_row * cl_dev, cl_dev, code, coupling_of, out_ref, wide_ref)
    for copy in others:
        copy.wait()


def side_operator_kernel(n_grp, n_row, cl_dev, cols_ref, rows_ref, live_ref, rest_ref, *refs):
    out_ref, wide_ref = refs
    per = rest_ref.shape[0] // 2

    def outer(ref):
        return jnp.concatenate([ref[:, :per], ref[:, 2 * per :]], axis=1)

    code = slot_codes(
        n_grp, n_row, cl_dev, 1, outer(cols_ref), outer(rows_ref), outer(live_ref)
    )

    def coupling_of(step):
        return rest_ref[:, step * 2 * LANES : (step + 1) * 2 * LANES]

    sum_slots(2, n_row * cl_dev, cl_dev, code, coupling_of, out_ref, wide_ref)


def far_pieces(total, pieces, pairs_piece):
    lane = lax.broadcasted_iota(jnp.int32, (K, LANES), 1)
    first = lane < K
    for operator_ref, base, piece_ref, places in pieces:
        for at, place in enumerate(places):
            for pair in range(pairs_piece):
                both = piece_ref[pl.ds((at * pairs_piece + pair) * K, K), :]
                swapped = jnp.concatenate([both[:, K:], both[:, :K]], axis=1)
                zero = jnp.zeros_like(both)
                weights = jnp.concatenate(
                    [
                        jnp.where(first, both, zero),
                        jnp.where(first, zero, swapped),
                        jnp.where(first, swapped, zero),
                        jnp.where(first, zero, both),
                    ],
                    axis=0,
                )
                index = base + place * pairs_piece + pair
                total = total + jnp.dot(
                    operator_ref[index], weights, preferred_element_type=F32
                )
    return total


def far_kernel(plan, pairs_piece, started, *refs):
    out_ref = refs[-1]
    total = refs[-2][...] if started else jnp.zeros(out_ref.shape, F32)
    pieces = [(refs[o], base, refs[p], places) for o, base, p, places in plan]
    out_ref[...] = far_pieces(total, pieces, pairs_piece)


def near_kernel(signal_ref, near_ref, basis_ref, total_ref, spread_ref):
    cl_dev = signal_ref.shape[0]
    for c in range(cl_dev):
        total = dot_nt(signal_ref[c], near_ref[c, 1])
        if c > 0:
            total = total + dot_nt(signal_ref[c - 1], near_ref[c, 0])
        if c < cl_dev - 1:
            total = total + dot_nt(signal_ref[c + 1], near_ref[c, 2])
        total_ref[:, c * LANES : (c + 1) * LANES] = total
    spread_ref[...] = jnp.zeros_like(spread_ref)
    for c in range(cl_dev):
        wide = basis_ref[c].astype(F32).reshape(TILES, HALVES, LANES)
        for parity in range(HALVES):
            start = parity * cl_dev * TILES + c * TILES
            spread_ref[start : start + TILES, c * LANES : (c + 1) * LANES] = wide[:, parity].astype(BF16)


def final_kernel(plan, pairs_piece, n_row, n_grp, *refs):
    other_ref, partner_ref, along_ref, across_ref, near_ref = refs[1:6]
    far_ref, near_total_ref, spread_ref, out_ref = refs[-4:]
    cl_dev = out_ref.shape[0]
    row = lax.axis_index("row")
    group = lax.axis_index("grp")
    odd = (row & 1) == 1
    odd_group = (group & 1) == 1
    from_other = other_ref[other_ref.shape[0] - R :]
    from_partner = partner_ref[partner_ref.shape[0] - R :]
    before = jnp.where(odd_group, from_partner, from_other)
    behind = jnp.where(odd_group, from_other, from_partner)
    along = jnp.where(row == 0, before, jnp.where(row == n_row - 1, behind, along_ref[...]))
    across = across_ref[...]
    zero = jnp.zeros_like(across)
    is_first = (row == 0) & (group == 0)
    is_last = (row == n_row - 1) & (group == n_grp - 1)
    low = jnp.where(is_first, zero, jnp.where(odd, across, along))
    high = jnp.where(is_last, zero, jnp.where(odd, along, across))
    sides = {0: dot_nt(low, near_ref[0, 0])}
    last = cl_dev - 1
    sides[last] = dot_nt(high, near_ref[last, 2])
    pieces = [(refs[o], base, refs[p], places) for o, base, p, places in plan]
    total = far_pieces(far_ref[...], pieces, pairs_piece)
    turned = total.T.astype(BF16)
    lhs = jnp.concatenate([turned[p * R : (p + 1) * R] for p in range(HALVES)], axis=1)
    res = near_total_ref[...] + jnp.dot(lhs, spread_ref[...], preferred_element_type=F32)
    for c in range(cl_dev):
        here = res[:, c * LANES : (c + 1) * LANES]
        if c in sides:
            here = here + sides[c]
        out_ref[c] = here.astype(BF16)


def held(*values):
    return [pltpu.with_memory_space_constraint(v, pltpu.VMEM) for v in values]


def per_device(signal, leaf_basis, near_blocks, coupling, block_cols, block_rows, block_live):
    cl_dev = signal.shape[0]
    n_row = lax.axis_size("row")
    n_grp = lax.axis_size("grp")
    gc = cl_dev * n_row
    pairs_piece = cl_dev // 2
    pairs_kind = gc // 2
    height = cl_dev * TILES

    def across_row(value, bit):
        return lax.ppermute(value, "row", [(i, i ^ bit) for i in range(n_row)])

    partners = [(i, i ^ 1) for i in range(n_grp)]
    others = [(i, (i + 1) % n_grp if i % 2 else (i - 1) % n_grp) for i in range(n_grp)]
    n_slots = coupling.shape[0]

    signal, leaf_basis, cols, rows, live, mine, for_across, for_along = call(
        skeleton_kernel,
        [(signal.shape, BF16), (leaf_basis.shape, BF16)]
        + [((1, n_slots), jnp.int32)] * 3
        + [((cl_dev // 2 * K, LANES), BF16), ((R, LANES), BF16), ((R, LANES), BF16)],
        signal,
        leaf_basis,
        block_cols[None],
        block_rows[None],
        block_live[None],
        in_hbm=range(5),
        scratch=[pltpu.SemaphoreType.DMA((5,))],
    )

    def wide(n_kinds):
        return (n_kinds * gc * (height + PAD) + height, LANES)

    own_operator, rest = call(
        functools.partial(own_operator_kernel, n_grp, n_row, cl_dev),
        [
            ((pairs_kind, height, 2 * LANES), BF16),
            ((n_slots // 3 * 2, coupling.shape[1]), BF16),
        ],
        cols,
        rows,
        live,
        coupling,
        in_hbm=(3,),
        scratch=[
            pltpu.VMEM((n_slots // 3, coupling.shape[1]), BF16),
            pltpu.VMEM(wide(1), F32),
            pltpu.SemaphoreType.DMA((4,)),
        ],
        room=wide(1)[0] * LANES * 4 + n_slots // 3 * coupling.shape[1] * 2,
    )
    side_operator = call(
        functools.partial(side_operator_kernel, n_grp, n_row, cl_dev),
        [((2 * pairs_kind, height, 2 * LANES), BF16)],
        cols,
        rows,
        live,
        rest,
        scratch=[pltpu.VMEM(wide(2), F32)],
        room=wide(2)[0] * LANES * 4,
    )
    (near_blocks,) = held(near_blocks)
    near_total, spread = call(
        near_kernel,
        [((R, cl_dev * LANES), F32), ((HALVES * height, cl_dev * LANES), BF16)],
        signal,
        near_blocks,
        leaf_basis,
    )

    row = lax.axis_index("row")

    def packed(*values):
        return jnp.concatenate(values, axis=0)

    row = lax.axis_index("row")

    def packed(*values):
        return jnp.concatenate(values, axis=0)

    places = [0]
    panel = mine
    along = for_along
    bit = n_row // 2
    while bit > 4:
        size = panel.shape[0]
        got = across_row(packed(panel, along), bit)
        panel = packed(panel, got[:size])
        crosses = (row % bit == 0) | (row % bit == bit - 1)
        along = jnp.where(crosses, got[size:], along)
        places = places + [p ^ bit for p in places]
        bit //= 2
    size = panel.shape[0]
    got = across_row(panel, 4)
    with_along = packed(panel, along)
    near_z = across_row(with_along, 2)
    far_z = across_row(with_along, 6)
    places = places + [p ^ 4 for p in places]
    places = places + [p ^ 2 for p in places]
    first_half = packed(panel, got)
    got = across_row(packed(first_half, for_across), 1)
    over_ya, across = got[: 2 * size], got[2 * size :]
    other_a = lax.ppermute(first_half, "grp", others)
    panel = packed(first_half, near_z[:size], far_z[:size])
    along = jnp.where((row % 4 == 1) | (row % 4 == 2), far_z[size:], near_z[size:])
    size = panel.shape[0] // 2
    places_y = [p ^ 1 for p in places]
    half = len(places) // 2
    got = across_row(packed(panel[size:], along), 1)
    leaps = [
        (g * n_row + r, h * n_row + (r ^ 1)) for g, h in others for r in range(n_row)
    ]
    other_b = lax.ppermute(packed(panel[size:], along), ("grp", "row"), leaps)
    over_yb, along = got[:size], got[size:]
    early_part = packed(panel, over_ya)
    early_places = places + places_y[:half]
    late_places = places_y[half:]
    other_c = lax.ppermute(over_ya, "grp", others)
    other_e = across_row(other_a, 2)
    plan = [
        (0, 0, 2, early_places),
        (0, 0, 3, late_places),
        (1, pairs_kind, 4, places[:half]),
        (1, pairs_kind, 5, places_y[:half]),
    ]
    own_far = call(
        functools.partial(far_kernel, plan, pairs_piece, False),
        [((height, LANES), F32)],
        own_operator,
        side_operator,
        *held(early_part, over_yb, other_a, other_c),
    )
    partner = lax.ppermute(packed(early_part, over_yb, along), "grp", partners)

    plan = [(0, 0, 1, early_places + late_places), (0, pairs_kind, 2, places[half:])]
    far = call(
        functools.partial(far_kernel, plan, pairs_piece, True),
        [((height, LANES), F32)],
        side_operator,
        *held(partner, other_e),
        own_far,
    )
    return pl.pallas_call(
        functools.partial(
            final_kernel, [(0, pairs_kind, 1, late_places)], pairs_piece, n_row, n_grp
        ),
        out_shape=jax.ShapeDtypeStruct(signal.shape, BF16),
        in_specs=[pl.BlockSpec(memory_space=pltpu.VMEM)] * 9,
        out_specs=pl.BlockSpec(memory_space=pltpu.VMEM),
        compiler_params=pltpu.CompilerParams(vmem_limit_bytes=4 << 20),
        name="final",
    )(
        side_operator,
        *held(other_b, partner, along, across),
        near_blocks,
        far,
        near_total,
        spread,
    )


def solution(mesh):
    in_specs = (
        P(("grp", "row"), None, None),
        P(("grp", "row"), None, None),
        P(("grp", "row"), None, None, None),
        P(("grp", "row"), None),
        P(("grp", "row")),
        P(("grp", "row")),
        P(("grp", "row")),
    )
    out_specs = P(("grp", "row"), None, None)

    return jax.shard_map(
        per_device, mesh=mesh, in_specs=in_specs, out_specs=out_specs, check_vma=False
    )
```
